32 devices in a mesh: dp: 16 (over z, y, x), seq: 2 (over core).
Axes of the slice: x: 2, y: 2, z: 4, core: 2. Of those that a mesh axis runs over, the one named last changes fastest.
Arguments:
- latents: float32 [2, 16, 256, 16], P(None, 'dp', 'seq'), may hold values from -6 to 6
- noises: float32 [2, 16, 256, 16], P(None, 'dp', 'seq'), may hold values from -6 to 6
- labels: int32 [2, 16], P(None, 'dp'), may hold values from 0 to 999
- dropped: int32 [2, 16], P(None, 'dp'), may hold values 0 or 1
- timesteps: int32 [2, 16], P(None, 'dp'), may hold values from 0 to 999
- layer_in: float32 [1, 1024, 14336], P(None, ('dp', 'seq'))
- layer_out: float32 [1, 4096, 1024], P(None, ('dp', 'seq')), may hold values from -0.09375 to 0.09375
- cond_table: float32 [4361, 1024], P(None, ('dp', 'seq'))
- bias_rows: float32 [19, 1024], P(None, ('dp', 'seq')), may hold values from -1.8 to 1.8
- head_bias: float32 [16], replicated, may hold values from -1.8 to 1.8
- layer_in_m: float32 [1, 1024, 14336], P(None, ('dp', 'seq')), may hold values from -7.1525574e-07 to 7.1525574e-07
- layer_in_v: float32 [1, 1024, 14336], P(None, ('dp', 'seq')), may hold values from 5.351141e-16 to 8.561826e-15
- layer_out_m: float32 [1, 4096, 1024], P(None, ('dp', 'seq')), may hold values from -7.1525574e-07 to 7.1525574e-07
- layer_out_v: float32 [1, 4096, 1024], P(None, ('dp', 'seq')), may hold values from 5.351141e-16 to 8.561826e-15
- cond_table_m: float32 [4361, 1024], P(None, ('dp', 'seq')), may hold values from -7.1525574e-07 to 7.1525574e-07
- cond_table_v: float32 [4361, 1024], P(None, ('dp', 'seq')), may hold values from 5.351141e-16 to 8.561826e-15
- bias_rows_m: float32 [19, 1024], P(None, ('dp', 'seq')), may hold values from -2.861023e-06 to 2.861023e-06
- bias_rows_v: float32 [19, 1024], P(None, ('dp', 'seq')), may hold values from 8.561826e-15 to 1.3698922e-13
- head_bias_m: float32 [16], replicated, may hold values from -2.861023e-06 to 2.861023e-06
- head_bias_v: float32 [16], replicated, may hold values from 8.561826e-15 to 1.3698922e-13
- adam_step: int32 [1], replicated, may hold values from 1 to 20
Outputs:
- loss: float32 [], replicated
- grad_norm: float32 [], replicated
- layer_in_new: float32 [1, 1024, 14336], P(None, ('dp', 'seq'))
- layer_in_m_new: float32 [1, 1024, 14336], P(None, ('dp', 'seq'))
- layer_in_v_new: float32 [1, 1024, 14336], P(None, ('dp', 'seq'))
- layer_out_new: float32 [1, 4096, 1024], P(None, ('dp', 'seq'))
- layer_out_m_new: float32 [1, 4096, 1024], P(None, ('dp', 'seq'))
- layer_out_v_new: float32 [1, 4096, 1024], P(None, ('dp', 'seq'))
- cond_table_new: float32 [4361, 1024], P(None, ('dp', 'seq'))
- cond_table_m_new: float32 [4361, 1024], P(None, ('dp', 'seq'))
- cond_table_v_new: float32 [4361, 1024], P(None, ('dp', 'seq'))
- bias_rows_new: float32 [19, 1024], P(None, ('dp', 'seq'))
- bias_rows_m_new: float32 [19, 1024], P(None, ('dp', 'seq'))
- bias_rows_v_new: float32 [19, 1024], P(None, ('dp', 'seq'))
- head_bias_new: float32 [16], replicated
- head_bias_m_new: float32 [16], replicated
- head_bias_v_new: float32 [16], replicated
The draws below stay inside these ranges and needn't reach their ends.
All inputs are finite; a program needn't handle non-finite values. No bound on the sum of `dropped` on one device may be relied on, other than what follows from the above.
Results may differ from the reference program's by a relative error of at most 0.0082.
Values may be sent and summed in bfloat16 or wider, within the bound.
A program may use at most 384 MiB of HBM per device.

```python
import math
import jax
import jax.numpy as jnp
from jax import lax

D = 1024
HEADS = 16
HEAD_DIM = 64
FF = 4096
CLASSES = 1000
FREQ = 256
PATCH = 16
GRID = 16
LAYERS = 1
MICRO = 2
IMG_DEV = 1
TOKENS_IMG = 256
IMG_MB = 16
WIDE = 14336
ROWS = 4361
NBIAS = 19
PARAMS = 23359504
N_DP = 16


def draw_layer_in(key, part):
    base = jax.random.normal(key, (LAYERS, D, 10 * D + FF), jnp.float32)
    column = jnp.arange(10 * D + FF)
    output_cols = (column >= 3 * D) & (column < 4 * D)
    factor = jnp.where(output_cols, 0.5 * GRID, 1.0)
    return base * factor[None, None, :] / math.sqrt(D)


def draw_cond_table(key, part):
    total = CLASSES + 1 + FREQ + 3 * D + 2 * PATCH
    base = jax.random.normal(key, (total, D), jnp.float32)
    places = jnp.arange(total)[:, None]
    end_class = CLASSES + 1
    end_time_one = end_class + FREQ
    end_time_two = end_time_one + D
    end_patch = end_time_two + PATCH
    factor = jnp.where(places < end_class, 0.2, jnp.where(places < end_time_one, 1.0 / math.sqrt(FREQ), jnp.where(places < end_time_two, 1.0 / math.sqrt(D), jnp.where(places < end_patch, 1.0 / math.sqrt(PATCH), 1.0 / math.sqrt(D)))))
    return base * factor


def place_ends(drawn, stream_key, smallest, largest):
    extent = drawn.shape
    place = [jax.random.randint(jax.random.fold_in(stream_key, axis), (), 0, extent[axis]) for axis in range(len(extent))]
    drawn = drawn.at[tuple(place)].set(smallest)
    longest = extent.index(max(extent))
    place[longest] = (place[longest] + 1) % extent[longest]
    return drawn.at[tuple(place)].set(largest)


def block_scale(stream_key, shape, shards, smallest, high):
    level, own = 1.0, jax.random.fold_in(stream_key, 6)
    for position, blocks in shards:
        draws = jnp.exp(jax.random.uniform(jax.random.fold_in(own, position), (blocks,), jnp.float32, smallest / len(shards), high / len(shards)))
        level = level * jnp.repeat(draws, shape[position] // blocks).reshape([-1 if axis == position else 1 for axis in range(len(shape))])
    return level


def gaussian(rng, shape, scale, limit, pieces=(), kind=jnp.bfloat16):
    factor_of = block_scale(rng, shape, pieces, -0.22, 0.18) if pieces else 1.0
    values = jax.random.normal(rng, shape, jnp.float32) * scale * factor_of
    return jnp.minimum(jnp.maximum(values, -limit), limit).astype(kind)


def setup_inputs(seed: int = 0) -> dict:
    splits = jax.random.split(jax.random.key(seed), 22)
    return {
        "latents": gaussian(splits[0], (MICRO, IMG_MB, TOKENS_IMG, PATCH), 1.0, 6.0, ((1, 16), (2, 2)), jnp.float32),
        "noises": gaussian(splits[1], (MICRO, IMG_MB, TOKENS_IMG, PATCH), 1.0, 6.0, ((1, 16), (2, 2)), jnp.float32),
        "labels": place_ends(jax.random.randint(splits[2], (MICRO, IMG_MB), 0, CLASSES), jax.random.fold_in(splits[2], 1), 0, CLASSES - 1).astype(jnp.int32),
        "dropped": place_ends((jax.random.randint(splits[3], (MICRO, IMG_MB), 0, 10) < 1).astype(jnp.int32), jax.random.fold_in(splits[3], 1), 0, 1),
        "timesteps": place_ends(jax.random.randint(splits[4], (MICRO, IMG_MB), 0, 1000), jax.random.fold_in(splits[4], 1), 0, 999).astype(jnp.int32),
        "layer_in": draw_layer_in(jax.random.fold_in(splits[21], 71), 0),
        "layer_out": gaussian(splits[6], (LAYERS, FF, D), FF ** -0.5, 0.09375, ((1, 32),), jnp.float32),
        "cond_table": draw_cond_table(jax.random.fold_in(splits[21], 71), 0),
        "bias_rows": gaussian(splits[8], (NBIAS, D), 0.3, 1.8, ((1, 32),), jnp.float32),
        "head_bias": gaussian(splits[9], (PATCH,), 0.3, 1.8, (), jnp.float32),
        "layer_in_m": gaussian(splits[10], (LAYERS, D, WIDE), (0.00055 / PARAMS ** 0.5), 7.152557373046875e-07, ((1, 32),), jnp.float32),
        "layer_in_v": jnp.clip(jnp.exp(math.log(8.561825971505413e-15) - 2.7725887 * jax.random.uniform(splits[11], (LAYERS, D, WIDE), jnp.float32) ** block_scale(splits[11], (LAYERS, D, WIDE), ((1, 32),), -0.2, 0.2)), 5.351141232190883e-16, 8.561825971505413e-15),
        "layer_out_m": gaussian(splits[12], (LAYERS, FF, D), (0.00055 / PARAMS ** 0.5), 7.152557373046875e-07, ((1, 32),), jnp.float32),
        "layer_out_v": jnp.clip(jnp.exp(math.log(8.561825971505413e-15) - 2.7725887 * jax.random.uniform(splits[13], (LAYERS, FF, D), jnp.float32) ** block_scale(splits[13], (LAYERS, FF, D), ((1, 32),), -0.2, 0.2)), 5.351141232190883e-16, 8.561825971505413e-15),
        "cond_table_m": gaussian(splits[14], (ROWS, D), (0.00055 / PARAMS ** 0.5), 7.152557373046875e-07, ((1, 32),), jnp.float32),
        "cond_table_v": jnp.clip(jnp.exp(math.log(8.561825971505413e-15) - 2.7725887 * jax.random.uniform(splits[15], (ROWS, D), jnp.float32) ** block_scale(splits[15], (ROWS, D), ((1, 32),), -0.2, 0.2)), 5.351141232190883e-16, 8.561825971505413e-15),
        "bias_rows_m": gaussian(splits[16], (NBIAS, D), (0.0022 / PARAMS ** 0.5), 2.86102294921875e-06, ((1, 32),), jnp.float32),
        "bias_rows_v": jnp.clip(jnp.exp(math.log(1.369892155440866e-13) - 2.7725887 * jax.random.uniform(splits[17], (NBIAS, D), jnp.float32) ** block_scale(splits[17], (NBIAS, D), ((1, 32),), -0.2, 0.2)), 8.561825971505413e-15, 1.369892155440866e-13),
        "head_bias_m": gaussian(splits[18], (PATCH,), (0.0022 / PARAMS ** 0.5), 2.86102294921875e-06, (), jnp.float32),
        "head_bias_v": jnp.clip(jnp.exp(jax.random.uniform(splits[19], (PATCH,), jnp.float32, math.log(8.561825971505413e-15), math.log(1.369892155440866e-13))), 8.561825971505413e-15, 1.369892155440866e-13),
        "adam_step": jax.random.randint(splits[20], (1,), 1, 21).astype(jnp.int32),
    }


@jax.custom_vjp
def low(v):
    return lax.optimization_barrier(v.astype(jnp.bfloat16)).astype(jnp.float32)

@jax.custom_vjp
def low_back(v):
    return v

def low_keep(v):
    return (low(v), None)

def low_pass(kept, grad):
    return (grad,)

def back_keep(v):
    return (v, None)

def back_low(kept, grad):
    return (low(grad),)
low.defvjp(low_keep, low_pass)
low_back.defvjp(back_keep, back_low)
highest = lax.Precision.HIGHEST
clip_limit = 0.005
rate = 0.05
decay = 0.01

def matmul(left, right):
    return jnp.dot(left, right, precision=highest)

def layer_norm(values):
    centred = values - lax.optimization_barrier(jnp.mean(values, axis=-1, keepdims=True))
    return centred * lax.rsqrt(lax.optimization_barrier(jnp.mean(centred * centred, axis=-1, keepdims=True)) + 1e-06)

def modulate(values, shift, scale):
    return layer_norm(values) * (1.0 + scale) + shift

def offsets():
    end_class = CLASSES + 1
    end_time_one = end_class + FREQ
    end_time_two = end_time_one + D
    end_patch = end_time_two + PATCH
    end_final = end_patch + 2 * D
    return (end_class, end_time_one, end_time_two, end_patch, end_final)

def positions(row_start, row_count):
    places = row_start + jnp.arange(row_count, dtype=jnp.int32)
    quarter = D // 4
    omegas = 1.0 / 10000.0 ** (jnp.arange(quarter, dtype=jnp.float32) / quarter)
    across = (places // GRID).astype(jnp.float32)[:, None] * omegas[None, :]
    along = (places % GRID).astype(jnp.float32)[:, None] * omegas[None, :]
    return jnp.concatenate([jnp.sin(across), jnp.cos(across), jnp.sin(along), jnp.cos(along)], axis=1)

def time_features(time_steps):
    half_freq = FREQ // 2
    rates = jnp.exp(-math.log(10000.0) * jnp.arange(half_freq, dtype=jnp.float32) / half_freq)
    angles = time_steps.astype(jnp.float32)[:, None] * rates[None, :]
    return jnp.concatenate([jnp.cos(angles), jnp.sin(angles)], axis=1)

def signal_levels(time_steps):
    angles = (time_steps.astype(jnp.float32) / 1000.0 + 0.008) / 1.008 * (math.pi / 2.0)
    levels = jnp.cos(angles) ** 2
    return (jnp.sqrt(levels), jnp.sqrt(1.0 - levels))

def block(hidden, cond_act, wide, narrow, rows):
    mods = low_back(matmul(cond_act, wide[:, 4 * D + FF:]) + rows[8:14].reshape(1, 6 * D))
    shift_a, scale_a, gate_a, shift_b, scale_b, gate_b = jnp.split(mods, 6, axis=1)
    normed = low(modulate(hidden, shift_a, scale_a))
    bias_qkv = jnp.concatenate([rows[0], jnp.zeros((D,), jnp.float32), rows[1]])
    packed = low(low_back(matmul(normed, wide[:, :3 * D]) + bias_qkv))
    queries = packed[:, :D].reshape(-1, HEADS, HEAD_DIM)
    keys = packed[:, D:2 * D].reshape(-1, HEADS, HEAD_DIM)
    values = packed[:, 2 * D:].reshape(-1, HEADS, HEAD_DIM)
    scores = low_back(jnp.einsum('qhd,khd->hqk', queries, keys, precision=highest) / math.sqrt(HEAD_DIM))
    weights = low(jax.nn.softmax(scores, axis=-1))
    attended = low(low_back(jnp.einsum('hqk,khd->qhd', weights, values, precision=highest).reshape(-1, D)))
    branch = low_back(matmul(attended, wide[:, 3 * D:4 * D]) + rows[2])
    middle = hidden + gate_a * branch
    normed = low(modulate(middle, shift_b, scale_b))
    upward = low_back(matmul(normed, wide[:, 4 * D:4 * D + FF]) + rows[3:7].reshape(1, FF))
    downward = low_back(matmul(low(jax.nn.gelu(upward, approximate=True)), narrow) + rows[7])
    return middle + gate_b * downward

def image_loss(weights, latent, noise_draw, class_id, drop_flag, time_step):
    wide_all, narrow_all, table, biases, bias_head = weights
    end_class, end_time_one, end_time_two, end_patch, end_final = offsets()
    bias_base = 14 * LAYERS
    keep_level, spread = signal_levels(time_step)
    noisy = low(keep_level * latent + spread * noise_draw)
    freqs = low(time_features(time_step[None]))
    time_one = low_back(matmul(freqs, table[end_class:end_time_one]) + biases[bias_base + 1])
    time_two = matmul(low(jax.nn.silu(time_one)), table[end_time_one:end_time_two]) + biases[bias_base + 2]
    chosen = jnp.where(drop_flag == 1, CLASSES, class_id)
    condition = low_back(time_two + table[chosen][None, :])
    cond_act = low(jax.nn.silu(condition))
    final_shift = low_back(matmul(cond_act, table[end_patch:end_patch + D]) + biases[bias_base + 3])
    final_scale = low_back(matmul(cond_act, table[end_patch + D:end_final]) + biases[bias_base + 4])
    hidden = low_back(matmul(noisy, table[end_time_two:end_patch]) + biases[bias_base]) + positions(0, TOKENS_IMG)
    for layer in range(LAYERS):
        hidden = block(hidden, cond_act, wide_all[layer], narrow_all[layer], biases[14 * layer:14 * layer + 14])
    normed = low(modulate(hidden, final_shift, final_scale))
    predicted = low_back(matmul(normed, table[end_final:].T) + bias_head)
    return jnp.sum((predicted - noise_draw) ** 2)

def adam(weight, grad, first_m, second_m, factor, step_count):
    clipped = grad * factor
    first_new = 0.9 * first_m + 0.1 * clipped
    second_new = 0.999 * second_m + 0.001 * clipped * clipped
    first_hat = first_new / (1.0 - 0.9 ** step_count)
    second_hat = second_new / (1.0 - 0.999 ** step_count)
    updated = weight - rate * (first_hat / (jnp.sqrt(second_hat) + 1e-08) + decay * weight)
    return (updated, first_new, second_new)

def reference(latents, noises, labels, dropped, timesteps, layer_in, layer_out, cond_table, bias_rows, head_bias, layer_in_m, layer_in_v, layer_out_m, layer_out_v, cond_table_m, cond_table_v, bias_rows_m, bias_rows_v, head_bias_m, head_bias_v, adam_step):
    images = MICRO * IMG_DEV * N_DP
    group = 16
    batched = (latents.reshape(images // group, group, TOKENS_IMG, PATCH), noises.reshape(images // group, group, TOKENS_IMG, PATCH), labels.reshape(images // group, group), dropped.reshape(images // group, group), timesteps.reshape(images // group, group))

    def total_loss(wide_all, narrow_all, table, biases, bias_head):
        weights = (low(wide_all), low(narrow_all), low(table), low(biases), bias_head)

        def one_image(latent, noise_draw, class_id, drop_flag, time_step):
            return image_loss(weights, latent, noise_draw, class_id, drop_flag, time_step)

        def one_group(carry, inputs):
            latent, noise_draw, class_id, drop_flag, time_step = inputs
            return (carry + jnp.sum(jax.vmap(one_image)(latent, noise_draw, class_id, drop_flag, time_step)), None)
        total, _ = lax.scan(jax.checkpoint(one_group), jnp.zeros((), jnp.float32), batched)
        return total / (images * TOKENS_IMG * PATCH)
    loss, pullback = jax.vjp(total_loss, layer_in, layer_out, cond_table, bias_rows, head_bias)
    grads = pullback(jnp.ones((), jnp.float32))
    norm = jnp.sqrt(sum((jnp.sum(grad * grad) for grad in grads)))
    factor = jnp.minimum(1.0, clip_limit / (norm + 1e-06))
    step_count = adam_step[0].astype(jnp.float32)
    results = [loss, norm]
    groups = ((layer_in, layer_in_m, layer_in_v), (layer_out, layer_out_m, layer_out_v), (cond_table, cond_table_m, cond_table_v), (bias_rows, bias_rows_m, bias_rows_v), (head_bias, head_bias_m, head_bias_v))
    for (weight, first_m, second_m), grad in zip(groups, grads):
        results.extend(adam(weight, grad, first_m, second_m, factor, step_count))
    return tuple(results)
```

```python
from functools import partial
import math

import jax
import jax.numpy as jnp
from jax import lax
from jax.experimental import pallas as pl
from jax.experimental.pallas import tpu as pltpu
from jax.sharding import PartitionSpec as P

D = 1024
HEADS = 16
HEAD_DIM = 64
FF = 4096
CLASSES = 1000
FREQ = 256
PATCH = 16
GRID = 16
MICRO = 2
TOKENS_IMG = 256
MAIN = 4 * D + FF
MODS = 6 * D

clip_limit = 0.005
rate = 0.05
decay = 0.01

BOTH = ("dp", "seq")
END_CLASS = CLASSES + 1
END_T1 = END_CLASS + FREQ
END_T2 = END_T1 + D
END_PATCH = END_T2 + PATCH
END_FINAL = END_PATCH + 2 * D


def low(values):
    return values.astype(jnp.bfloat16)


def mm(left, right):
    return jnp.dot(left, right, preferred_element_type=jnp.float32)


def mm_tn(left, right):
    return lax.dot_general(
        left, right, (((0,), (0,)), ((), ())), preferred_element_type=jnp.float32
    )


def mm_nt(left, right):
    return lax.dot_general(
        left, right, (((1,), (1,)), ((), ())), preferred_element_type=jnp.float32
    )


def positions():
    places = jnp.arange(TOKENS_IMG, dtype=jnp.int32)
    quarter = D // 4
    omegas = 1.0 / 10000.0 ** (jnp.arange(quarter, dtype=jnp.float32) / quarter)
    across = (places // GRID).astype(jnp.float32)[:, None] * omegas[None, :]
    along = (places % GRID).astype(jnp.float32)[:, None] * omegas[None, :]
    return jnp.concatenate(
        [jnp.sin(across), jnp.cos(across), jnp.sin(along), jnp.cos(along)], axis=1
    )


def time_features(time_steps):
    half_freq = FREQ // 2
    rates = jnp.exp(-math.log(10000.0) * jnp.arange(half_freq, dtype=jnp.float32) / half_freq)
    angles = time_steps.astype(jnp.float32)[:, None] * rates[None, :]
    return jnp.concatenate([jnp.cos(angles), jnp.sin(angles)], axis=1)


def signal_levels(time_steps):
    angles = (time_steps.astype(jnp.float32) / 1000.0 + 0.008) / 1.008 * (math.pi / 2.0)
    levels = jnp.cos(angles) ** 2
    return (jnp.sqrt(levels), jnp.sqrt(1.0 - levels))


def norm_stats(values):
    centred = values - jnp.mean(values, axis=-1, keepdims=True)
    inverse = lax.rsqrt(jnp.mean(centred * centred, axis=-1, keepdims=True) + 1e-06)
    return (centred * inverse, inverse)


def norm_back(grad, unit, inverse, scale):
    grad_unit = grad * (1.0 + scale)
    mean_one = jnp.mean(grad_unit, axis=-1, keepdims=True)
    mean_two = jnp.mean(grad_unit * unit, axis=-1, keepdims=True)
    grad_values = inverse * (grad_unit - mean_one - unit * mean_two)
    return (
        grad_values,
        jnp.sum(grad, axis=0, keepdims=True),
        jnp.sum(grad * unit, axis=0, keepdims=True),
    )


GELU_A = math.sqrt(2.0 / math.pi)
GELU_B = 0.044715


def gelu_both(values):
    squared = values * values
    bent = jnp.tanh(GELU_A * (values + GELU_B * squared * values))
    out = 0.5 * values * (1.0 + bent)
    slope = 0.5 * (1.0 + bent) + 0.5 * values * (1.0 - bent * bent) * (
        GELU_A * (1.0 + 3.0 * GELU_B * squared)
    )
    return (out, slope)


def silu_slope(values):
    sig = jax.nn.sigmoid(values)
    return sig * (1.0 + values * (1.0 - sig))


def heads_of(values):
    return values.reshape(values.shape[0], HEADS, HEAD_DIM)


def adam(weight, grad, first_m, second_m, factor, step_count):
    clipped = grad * factor
    first_new = 0.9 * first_m + 0.1 * clipped
    second_new = 0.999 * second_m + 0.001 * clipped * clipped
    first_hat = first_new / (1.0 - 0.9**step_count)
    second_hat = second_new / (1.0 - 0.999**step_count)
    updated = weight - rate * (first_hat / (jnp.sqrt(second_hat) + 1e-08) + decay * weight)
    return (updated, first_new, second_new)


ID_TYPE = pl.DeviceIdType.MESH
NEAR_LAG, FAR_LAG, BOTH_LAG, HOP, RS_LAG = 0, 1, 2, 1, 1
LINE = 4


def route():
    me, core = lax.axis_index("dp"), lax.axis_index("seq")
    x, y, z = me % 2, (me // 2) % 2, me // 4
    step_x, step_y = 1 - 2 * x, 2 - 4 * y
    near = me + (1 - core) * step_y + core * step_x
    far = me + (1 - core) * step_x + core * step_y
    both = me + step_x + step_y

    def along(chip, hops):
        return chip + 4 * ((z + hops) % LINE - z)

    return me, core, near, far, both, along


def greet(me, core, near, far, along):
    barrier = pltpu.get_barrier_semaphore()
    peers = [(along(me, k), core) for k in range(1, LINE)]
    peers += [(near, core), (far, core), (me, 1 - core)]
    for peer in peers:
        pl.semaphore_signal(barrier, inc=1, device_id=peer, device_id_type=ID_TYPE)
    pl.semaphore_wait(barrier, len(peers))


def gather_kernel(pieces, *refs):
    count = (len(refs) - 3) // 2
    shards, wholes = refs[:count], refs[count : 2 * count]
    send_sem, recv_sem, own_sem = refs[2 * count :]
    me, core, near, far, both, along = route()

    lines = [me] + [along(me, -k) for k in range(1, LINE)]
    from_near = [near] + [along(near, -k) for k in range(1, LINE)]
    from_far = [far] + [along(far, -k) for k in range(1, LINE)]
    from_both = [both] + [along(both, -k) for k in range(1, LINE)]
    sends = []

    def copy_of(piece, slot, chip, core_of, target, own=False):
        which, cut = pieces[piece]
        there = wholes[which].at[(2 * chip + core_of, *cut)]
        return pltpu.make_async_remote_copy(
            src_ref=shards[which].at[cut] if own else there,
            dst_ref=there,
            send_sem=send_sem.at[piece, slot],
            recv_sem=recv_sem.at[piece, slot],
            device_id=target,
            device_id_type=ID_TYPE,
        )

    def send(piece, slot, chip, target, own=False):
        copy = copy_of(piece, slot, chip, core, target, own)
        copy.start()
        sends.append(copy)

    def arrive(piece, slot, chip, core_of):
        copy_of(piece, slot, chip, core_of, (me, 1 - core)).wait_recv()

    to_next, to_near, to_far, to_core = (along(me, 1), core), (near, core), (far, core), (me, 1 - core)

    def start(piece):
        send(piece, 0, me, to_next, own=True)
        send(piece, 3, me, to_near, own=True)
        send(piece, 7, me, to_far, own=True)
        send(piece, 15, me, to_core, own=True)

    def from_line(k):
        def step(piece):
            arrive(piece, k - 1, lines[k], core)
            if k + 1 < LINE:
                send(piece, k, lines[k], to_next)
            send(piece, 3 + k, lines[k], to_near)
            send(piece, 7 + k, lines[k], to_far)
            send(piece, 15 + k, lines[k], to_core)

        return (HOP * (k - 1), step)

    def by_near(k):
        def step(piece):
            arrive(piece, 3 + k, from_near[k], core)
            send(piece, 11 + k, from_near[k], to_far)
            send(piece, 19 + k, from_near[k], to_core)

        return (HOP * max(k, 1) + NEAR_LAG, step)

    def by_far(k):
        def step(piece):
            arrive(piece, 7 + k, from_far[k], core)
            send(piece, 23 + k, from_far[k], to_core)

        return (HOP * max(k, 1) + FAR_LAG, step)

    def by_both(k):
        def step(piece):
            arrive(piece, 11 + k, from_both[k], core)
            send(piece, 27 + k, from_both[k], to_core)

        return (HOP * max(k, 1) + BOTH_LAG, step)

    def by_core(piece):
        for group, chips in enumerate((lines, from_near, from_far, from_both)):
            for k in range(LINE):
                arrive(piece, 15 + 4 * group + k, chips[k], 1 - core)

    steps = [from_line(k) for k in range(1, LINE)]
    steps += [by_near(k) for k in range(LINE)]
    steps += [by_far(k) for k in range(LINE)]
    steps += [by_both(k) for k in range(LINE)]
    steps.append((HOP * LINE + BOTH_LAG, by_core))

    greet(me, core, near, far, along)
    total = len(pieces)
    for piece in range(total):
        start(piece)
    own = [
        pltpu.make_async_copy(shard, whole.at[2 * me + core], own_sem.at[i])
        for i, (shard, whole) in enumerate(zip(shards, wholes))
    ]
    for copy in own:
        copy.start()
    for turn in range(total + steps[-1][0]):
        for late, step in steps:
            if 0 <= turn - late < total:
                step(turn - late)
    for copy in sends:
        copy.wait_send()
    for copy in own:
        copy.wait()


def gather_weights(shards, n_dev, pieces):
    count = len(shards)
    return pl.pallas_call(
        partial(gather_kernel, pieces),
        out_shape=[jax.ShapeDtypeStruct((n_dev, *s.shape), s.dtype) for s in shards],
        in_specs=[pl.BlockSpec(memory_space=pl.ANY)] * count,
        out_specs=[pl.BlockSpec(memory_space=pl.ANY)] * count,
        scratch_shapes=[
            pltpu.SemaphoreType.DMA((len(pieces), 31)),
            pltpu.SemaphoreType.DMA((len(pieces), 31)),
            pltpu.SemaphoreType.DMA((count,)),
        ],
        compiler_params=pltpu.CompilerParams(collective_id=0, has_side_effects=True),
    )(*shards)


def scatter_kernel(pieces, count, *refs):
    parts, outs = refs[:count], refs[count : 2 * count]
    held, from_core, from_far, from_near, from_line = (
        refs[(2 + i) * count : (3 + i) * count] for i in range(5)
    )
    send_sem, recv_sem, load_sem = refs[7 * count :]
    me, core, near, far, both, along = route()
    chips = [along(chip, -k) for chip in (me, near, far, both) for k in range(LINE)]
    others = [along(chip, -k) for chip in (me, far, near, both) for k in range(LINE)]
    sends = []

    def send(piece, slot, source, target_ref, target):
        copy = pltpu.make_async_remote_copy(
            src_ref=source,
            dst_ref=target_ref,
            send_sem=send_sem.at[piece, slot],
            recv_sem=recv_sem.at[piece, slot],
            device_id=target,
            device_id_type=ID_TYPE,
        )
        copy.start()
        sends.append(copy)

    def arrive(piece, slot, target_ref):
        pltpu.make_async_remote_copy(
            src_ref=target_ref,
            dst_ref=target_ref,
            send_sem=send_sem.at[piece, slot],
            recv_sem=recv_sem.at[piece, slot],
            device_id=(me, 1 - core),
            device_id_type=ID_TYPE,
        ).wait_recv()

    def view(refs_of, piece, j):
        which, cut = pieces[piece]
        return refs_of[which].at[(j, *cut)]

    def load(piece, j):
        which, cut = pieces[piece]
        return pltpu.make_async_copy(
            parts[which].at[(2 * chips[j] + core, *cut)],
            view(held, piece, j),
            load_sem.at[piece, j],
        )

    def add(piece, j, other):
        mine = view(held, piece, j)
        total = mine[...].astype(jnp.float32) + other[...].astype(jnp.float32)
        mine[...] = total.astype(jnp.bfloat16)

    order = [12 + k for k in (1, 2, 3, 0)] + [8 + k for k in (1, 2, 3, 0)]
    order += [4 + k for k in (1, 2, 3, 0)] + [k for k in (1, 2, 3, 0)]

    def begin(piece):
        which, cut = pieces[piece]
        for j in order:
            send(
                piece,
                j,
                parts[which].at[(2 * others[j] + 1 - core, *cut)],
                view(from_core, piece, j),
                (me, 1 - core),
            )
            load(piece, j).start()

    def by_core(piece):
        for j in order:
            load(piece, j).wait()
            arrive(piece, j, view(from_core, piece, j))
            add(piece, j, view(from_core, piece, j))
            if j >= 8:
                send(piece, 16 + j - 8, view(held, piece, j), view(from_far, piece, j - 8), (far, core))

    def by_far(piece):
        for j in order[8:]:
            arrive(piece, 16 + j, view(from_far, piece, j))
            add(piece, j, view(from_far, piece, j))
            if j >= 4:
                send(piece, 24 + j - 4, view(held, piece, j), view(from_near, piece, j - 4), (near, core))

    def by_near(piece):
        for j in order[12:]:
            arrive(piece, 24 + j, view(from_near, piece, j))
            add(piece, j, view(from_near, piece, j))
            if j:
                send(piece, 27 + j, view(held, piece, j), view(from_line, piece, j - 1), (along(me, -j), core))

    def by_line(piece):
        which, cut = pieces[piece]
        total = view(held, piece, 0)[...].astype(jnp.float32)
        for j in range(1, LINE):
            arrive(piece, 27 + j, view(from_line, piece, j - 1))
            total = total + view(from_line, piece, j - 1)[...].astype(jnp.float32)
        outs[which][cut] = total

    greet(me, core, near, far, along)
    total = len(pieces)
    for piece in range(total):
        begin(piece)
    steps = [(0, by_core), (RS_LAG, by_far), (2 * RS_LAG, by_near), (3 * RS_LAG, by_line)]
    for turn in range(total + steps[-1][0]):
        for late, step in steps:
            if 0 <= turn - late < total:
                step(turn - late)
    for copy in sends:
        copy.wait_send()


def scatter_grads(parts, pieces, call_id):
    count = len(parts)
    shards = [p.shape[1:] for p in parts]
    return pl.pallas_call(
        partial(scatter_kernel, pieces, count),
        out_shape=[jax.ShapeDtypeStruct(s, jnp.float32) for s in shards],
        in_specs=[pl.BlockSpec(memory_space=pl.ANY)] * count,
        out_specs=[pl.BlockSpec(memory_space=pltpu.VMEM)] * count,
        scratch_shapes=[
            *(pltpu.VMEM((blocks, *s), jnp.bfloat16) for blocks in (16, 16, 8, 4, 3) for s in shards),
            pltpu.SemaphoreType.DMA((len(pieces), 31)),
            pltpu.SemaphoreType.DMA((len(pieces), 31)),
            pltpu.SemaphoreType.DMA((len(pieces), 16)),
        ],
        compiler_params=pltpu.CompilerParams(
            collective_id=call_id, has_side_effects=True, vmem_limit_bytes=56 * 2**20
        ),
    )(*parts)


def exchange_kernel(kinds, n_dev, *refs):
    count = len(kinds)
    sources, outs = refs[:count], refs[count : 2 * count]
    send_sem, recv_sem = refs[2 * count :]
    me = 2 * lax.axis_index("dp") + lax.axis_index("seq")
    others = [(me + k) % n_dev for k in range(1, n_dev)]
    barrier = pltpu.get_barrier_semaphore()
    for other in others:
        pl.semaphore_signal(barrier, inc=1, device_id=(other // 2, other % 2), device_id_type=ID_TYPE)
    pl.semaphore_wait(barrier, n_dev - 1)

    def copy_of(i, k, other, block):
        return pltpu.make_async_remote_copy(
            src_ref=sources[i] if kinds[i] == "all" else sources[i].at[other],
            dst_ref=outs[i].at[block],
            send_sem=send_sem.at[i, k],
            recv_sem=recv_sem.at[i, k],
            device_id=(other // 2, other % 2),
            device_id_type=ID_TYPE,
        )

    copies = [copy_of(i, k, other, me) for k, other in enumerate(others) for i in range(count)]
    for copy in copies:
        copy.start()
    for i in range(count):
        outs[i][me] = sources[i][...] if kinds[i] == "all" else sources[i][me]
    for k in range(n_dev - 1):
        sender = (me + n_dev - 1 - k) % n_dev
        for i in range(count):
            copy_of(i, k, sender, sender).wait_recv()
    for copy in copies:
        copy.wait_send()


def exchange(arrays, kinds, n_dev, call_id):
    count = len(arrays)
    return pl.pallas_call(
        partial(exchange_kernel, kinds, n_dev),
        out_shape=[
            jax.ShapeDtypeStruct((n_dev, *a.shape) if kind == "all" else a.shape, a.dtype)
            for a, kind in zip(arrays, kinds)
        ],
        in_specs=[pl.BlockSpec(memory_space=pltpu.VMEM)] * count,
        out_specs=[pl.BlockSpec(memory_space=pltpu.VMEM)] * count,
        scratch_shapes=[
            pltpu.SemaphoreType.DMA((count, n_dev - 1)),
            pltpu.SemaphoreType.DMA((count, n_dev - 1)),
        ],
        compiler_params=pltpu.CompilerParams(
            collective_id=call_id, has_side_effects=True, vmem_limit_bytes=32 * 2**20
        ),
    )(*arrays)

def tiled(parts):
    return parts[0].shape[0] % 16 == 0 and lax.axis_size("dp") == 4 * LINE


def column_cuts(which, columns, step):
    return [(which, (slice(None), slice(c, c + step))) for c in range(0, columns, step)]


def row_cuts(which, rows, step):
    return [(which, (slice(r, r + step), slice(None))) for r in range(0, rows, step)]


def all_weights(main, narrow, n_dev):
    if not tiled([main, narrow]):
        return (
            lax.all_gather(main, BOTH, axis=0, tiled=True),
            lax.all_gather(narrow, BOTH, axis=0, tiled=True),
        )
    pieces = column_cuts(0, MAIN, 1024) + row_cuts(1, FF // n_dev, 32)
    main_all, narrow_all = gather_weights([main, narrow], n_dev, tuple(pieces))
    return main_all.reshape(D, MAIN), narrow_all.reshape(FF, D)


def summed_grads(parts, n_dev):
    blocks = [p.reshape(n_dev, p.shape[0] // n_dev, p.shape[1]) for p in parts]
    if not tiled([b[0] for b in blocks]):
        return [
            lax.psum_scatter(p, BOTH, scatter_dimension=0, tiled=True).astype(jnp.float32)
            for p in parts
        ]
    pieces = row_cuts(0, FF // n_dev, 32)
    for which in range(1, len(parts)):
        pieces += column_cuts(which, parts[which].shape[1], 1024)
    return scatter_grads(blocks, tuple(pieces), 1)


def swap(arrays, kinds, n_dev, call_id):
    if n_dev > 8 * LINE:
        return [
            lax.all_gather(a, BOTH) if kind == "all" else lax.all_to_all(a, BOTH, 0, 0, tiled=True)
            for a, kind in zip(arrays, kinds)
        ]
    return exchange(arrays, kinds, n_dev, call_id)


def shards(
    latents,
    noises,
    labels,
    dropped,
    timesteps,
    layer_in,
    layer_out,
    cond_table,
    bias_rows,
    head_bias,
    layer_in_m,
    layer_in_v,
    layer_out_m,
    layer_out_v,
    cond_table_m,
    cond_table_v,
    bias_rows_m,
    bias_rows_v,
    head_bias_m,
    head_bias_v,
    adam_step,
):
    core = lax.axis_index("seq")
    chips = lax.axis_size("dp")
    n_dev = chips * lax.axis_size("seq")
    me = lax.axis_index("dp") * 2 + core
    norm_count = float(MICRO * chips * TOKENS_IMG * PATCH)
    part = layer_in.shape[1]

    pair = jnp.concatenate([latents[:, 0], noises[:, 0]], axis=2)
    other = lax.dynamic_index_in_dim(pair, 1 - core, 0, keepdims=False)
    mine = lax.dynamic_index_in_dim(pair, core, 0, keepdims=False)
    came = lax.ppermute(other, "seq", [(0, 1), (1, 0)])
    image = jnp.where(core == 0, jnp.concatenate([mine, came]), jnp.concatenate([came, mine]))
    latent, noise = image[:, :PATCH], image[:, PATCH:]

    scalars = jnp.stack([labels[:, 0], dropped[:, 0], timesteps[:, 0]], axis=1)
    scalars = lax.dynamic_slice_in_dim(scalars, core, 1, 0).astype(jnp.float32)
    scalars = jnp.pad(scalars, ((0, 0), (0, 125)))

    main_low = low(layer_in[0, :, :MAIN])
    ada_low = low(layer_in[0, :, MAIN:])
    narrow_low = low(layer_out[0])
    table_low = low(cond_table)
    bias_low = low(bias_rows)
    bias_own = bias_low.astype(jnp.float32)

    small = jnp.concatenate([bias_low, table_low[END_T2:END_PATCH], table_low[END_FINAL:]], axis=0)
    small_all, scalars = swap([small, scalars], ("all", "all"), n_dev, 2)
    small_all = jnp.transpose(small_all, (1, 0, 2)).reshape(-1, D)
    scalars = scalars[:, 0, :3].astype(jnp.int32)
    chosen = jnp.where(scalars[:, 1] == 1, CLASSES, scalars[:, 0])
    times = scalars[:, 2]
    my_time = lax.dynamic_slice_in_dim(times, me, 1)
    bias_all = small_all[:19].astype(jnp.float32)
    patch_w = small_all[19:35]
    out_w = small_all[35:51]
    main_all, narrow_all = all_weights(main_low, narrow_low, n_dev)

    freqs = low(time_features(times))
    time_one = mm(freqs, table_low[END_CLASS:END_T1]) + bias_own[15]
    time_act = low(jax.nn.silu(time_one))
    (time_act_all,) = swap([time_act], ("all",), n_dev, 3)
    time_act_all = jnp.transpose(time_act_all, (1, 0, 2)).reshape(n_dev, D)
    choose = low((chosen[:, None] == jnp.arange(CLASSES + 1, dtype=jnp.int32)[None, :]))
    condition = (
        mm(time_act_all, table_low[END_T1:END_T2])
        + bias_own[16]
        + mm(choose, table_low[:END_CLASS])
    )
    cond_act = low(jax.nn.silu(condition))
    mods_part = low(mm(cond_act, ada_low)).reshape(n_dev, MODS // 128, 128)
    cond_act_all, mods_came = swap([cond_act, mods_part], ("all", "each"), n_dev, 4)
    cond_act_all = jnp.transpose(cond_act_all, (1, 0, 2)).reshape(n_dev, D)
    mods = (
        jnp.sum(mods_came.astype(jnp.float32), axis=0).reshape(1, MODS)
        + bias_all[8:14].reshape(1, MODS)
    )
    final_cols = jnp.concatenate(
        [
            mm(cond_act_all, table_low[END_PATCH : END_PATCH + D]) + bias_own[17],
            mm(cond_act_all, table_low[END_PATCH + D : END_FINAL]) + bias_own[18],
        ],
        axis=1,
    )
    (final_came,) = swap([final_cols[:, None]], ("each",), n_dev, 5)
    final_came = final_came[:, 0]
    f_shift = final_came[:, :part].reshape(1, D)
    f_scale = final_came[:, part:].reshape(1, D)
    shift_a, scale_a, gate_a, shift_b, scale_b, gate_b = jnp.split(mods, 6, axis=1)

    keep_level, spread = signal_levels(my_time)
    noisy = low(keep_level[:, None] * latent + spread[:, None] * noise)
    hidden = mm(noisy, patch_w) + bias_all[14] + positions()
    unit_a, inv_a = norm_stats(hidden)
    normed_a = low(unit_a * (1.0 + scale_a) + shift_a)
    bias_qkv = jnp.concatenate([bias_all[0], jnp.zeros((D,), jnp.float32), bias_all[1]])
    packed = low(mm(normed_a, main_all[:, : 3 * D]) + bias_qkv)
    queries, keys, values = (heads_of(packed[:, i * D : (i + 1) * D]) for i in range(3))
    head_scale = 1.0 / math.sqrt(HEAD_DIM)
    scores = (
        jnp.einsum("shd,khd->hsk", queries, keys, preferred_element_type=jnp.float32) * head_scale
    )
    expd = jnp.exp(scores - jnp.max(scores, axis=-1, keepdims=True))
    probs = expd / jnp.sum(expd, axis=-1, keepdims=True)
    probs_low = low(probs)
    attended = jnp.einsum("hsk,khd->shd", probs_low, values, preferred_element_type=jnp.float32)
    attended = low(attended.reshape(TOKENS_IMG, D))
    branch = mm(attended, main_all[:, 3 * D : 4 * D]) + bias_all[2]
    middle = hidden + gate_a * branch
    unit_b, inv_b = norm_stats(middle)
    normed_b = low(unit_b * (1.0 + scale_b) + shift_b)
    upward = mm(normed_b, main_all[:, 4 * D :]) + bias_all[3:7].reshape(FF)
    activated, slope = gelu_both(upward)
    activated = low(activated)
    downward = mm(activated, narrow_all) + bias_all[7]
    last = middle + gate_b * downward
    unit_f, inv_f = norm_stats(last)
    normed_f = low(unit_f * (1.0 + f_scale) + f_shift)
    predicted = mm_nt(normed_f, out_w) + head_bias

    differ = predicted - noise
    loss_part = jnp.sum(differ * differ) / norm_count
    grad_pred = low(2.0 * differ / norm_count)
    head_part = jnp.sum(grad_pred, axis=0, dtype=jnp.float32)
    grad_out_w = mm_tn(grad_pred, normed_f)
    grad_last, g_fshift, g_fscale = norm_back(mm(grad_pred, out_w), unit_f, inv_f, f_scale)
    g_gate_b = jnp.sum(grad_last * downward, axis=0, keepdims=True)
    grad_down = low(gate_b * grad_last)
    grad_narrow = low(mm_tn(activated, grad_down))
    grad_up = low(slope * mm_nt(grad_down, narrow_all))
    grad_fc1 = low(mm_tn(normed_b, grad_up))
    grad_mid, g_shift_b, g_scale_b = norm_back(
        mm_nt(grad_up, main_all[:, 4 * D :]), unit_b, inv_b, scale_b
    )
    grad_middle = grad_last + grad_mid
    g_gate_a = jnp.sum(grad_middle * branch, axis=0, keepdims=True)
    grad_branch = low(gate_a * grad_middle)
    grad_proj = low(mm_tn(attended, grad_branch))
    grad_att = heads_of(low(mm_nt(grad_branch, main_all[:, 3 * D : 4 * D])))
    grad_probs = jnp.einsum("shd,khd->hsk", grad_att, values, preferred_element_type=jnp.float32)
    grad_values = jnp.einsum("hsk,shd->khd", probs_low, grad_att, preferred_element_type=jnp.float32)
    grad_scores = low(
        probs * (grad_probs - jnp.sum(grad_probs * probs, axis=-1, keepdims=True))
    )
    grad_queries = (
        jnp.einsum("hsk,khd->shd", grad_scores, keys, preferred_element_type=jnp.float32)
        * head_scale
    )
    grad_keys = (
        jnp.einsum("hsk,shd->khd", grad_scores, queries, preferred_element_type=jnp.float32)
        * head_scale
    )
    grad_packed = low(
        jnp.concatenate(
            [g.reshape(TOKENS_IMG, D) for g in (grad_queries, grad_keys, grad_values)], axis=1
        )
    )
    grad_qkv = low(mm_tn(normed_a, grad_packed))
    grad_hid, g_shift_a, g_scale_a = norm_back(
        mm_nt(grad_packed, main_all[:, : 3 * D]), unit_a, inv_a, scale_a
    )
    grad_embed = low(grad_middle + grad_hid)
    grad_patch = mm_tn(noisy, grad_embed)

    grad_narrow, grad_fc1, grad_proj, grad_qkv = summed_grads(
        [grad_narrow, grad_fc1, grad_proj, grad_qkv], n_dev
    )

    mods_grads = low(
        jnp.concatenate(
            [g_shift_a, g_scale_a, g_gate_a, g_shift_b, g_scale_b, g_gate_b, g_fshift, g_fscale],
            axis=1,
        )
    )
    (mods_grads,) = swap([mods_grads.reshape(8 * D // 128, 128)], ("all",), n_dev, 6)
    mods_grads = mods_grads.reshape(n_dev, 8 * D)
    mods_low = mods_grads[:, :MODS]
    cut = mods_grads.reshape(n_dev, 8, n_dev, part)
    own_cols = lax.dynamic_index_in_dim(cut, me, 2, keepdims=False)
    fshift_low, fscale_low = own_cols[:, 6], own_cols[:, 7]
    grad_ada = mm_tn(cond_act, mods_low)
    cond_part = mm_nt(fshift_low, table_low[END_PATCH : END_PATCH + D]) + mm_nt(
        fscale_low, table_low[END_PATCH + D : END_FINAL]
    )
    (cond_came,) = swap([cond_part.reshape(n_dev, n_dev, part).transpose(1, 0, 2)], ("each",), n_dev, 7)
    grad_cond_act = jnp.sum(cond_came, axis=0) + mm_nt(mods_low, ada_low)
    grad_condition = low(grad_cond_act * silu_slope(condition))
    time_part = mm_nt(grad_condition, table_low[END_T1:END_T2])

    row_sums = lambda values: jnp.sum(values.astype(jnp.float32), axis=0, keepdims=True)
    packed_sums = row_sums(grad_packed)
    small_part = jnp.concatenate(
        [
            packed_sums[:, :D],
            packed_sums[:, 2 * D :],
            row_sums(grad_branch),
            row_sums(grad_up).reshape(4, D),
            row_sums(grad_down),
            row_sums(grad_embed),
            grad_patch,
            grad_out_w,
        ],
        axis=0,
    )
    rows_in = small_part.shape[0]
    sums_mine = jnp.pad(jnp.concatenate([loss_part[None], head_part]), (0, 111))[None]
    time_came, small_came, sums_all = swap(
        [
            time_part.reshape(n_dev, n_dev, part).transpose(1, 0, 2),
            small_part.reshape(rows_in, n_dev, part).transpose(1, 0, 2),
            sums_mine,
        ],
        ("each", "each", "all"),
        n_dev,
        8,
    )
    grad_time = low(jnp.sum(time_came, axis=0) * silu_slope(time_one))
    small_came = jnp.sum(small_came, axis=0)
    sums_all = jnp.sum(sums_all[:, 0, :17], axis=0)
    loss_total, head_total = sums_all[0], sums_all[1:]

    grad_table = jnp.concatenate(
        [
            mm_tn(choose, grad_condition),
            mm_tn(freqs, grad_time),
            mm_tn(time_act_all, grad_condition),
            small_came[9:25],
            mm_tn(cond_act_all, fshift_low),
            mm_tn(cond_act_all, fscale_low),
            small_came[25:41],
        ],
        axis=0,
    )
    grad_bias = jnp.concatenate(
        [
            small_came[:8],
            jnp.sum(own_cols[:, :6].astype(jnp.float32), axis=0),
            small_came[8:9],
            row_sums(grad_time),
            row_sums(grad_condition),
            row_sums(fshift_low),
            row_sums(fscale_low),
        ],
        axis=0,
    )
    grad_wide = jnp.concatenate([grad_qkv, grad_proj, grad_fc1, grad_ada], axis=1)[None]
    grad_narrow = grad_narrow[None]

    local_squares = (
        jnp.sum(grad_wide * grad_wide)
        + jnp.sum(grad_narrow * grad_narrow)
        + jnp.sum(grad_table * grad_table)
        + jnp.sum(grad_bias * grad_bias)
    )
    (squares,) = swap([jnp.full((1, 128), local_squares)], ("all",), n_dev, 9)
    squares = jnp.sum(squares[:, 0, 0])
    norm = jnp.sqrt(squares + jnp.sum(head_total * head_total))
    factor = jnp.minimum(1.0, clip_limit / (norm + 1e-06))
    step_count = adam_step[0].astype(jnp.float32)
    results = [loss_total, norm]
    results.extend(adam(layer_in, grad_wide, layer_in_m, layer_in_v, factor, step_count))
    results.extend(adam(layer_out, grad_narrow, layer_out_m, layer_out_v, factor, step_count))
    results.extend(adam(cond_table, grad_table, cond_table_m, cond_table_v, factor, step_count))
    results.extend(adam(bias_rows, grad_bias, bias_rows_m, bias_rows_v, factor, step_count))
    results.extend(adam(head_bias, head_total, head_bias_m, head_bias_v, factor, step_count))
    return tuple(results)


def solution(mesh):
    in_specs = (
        P(None, "dp", "seq", None),
        P(None, "dp", "seq", None),
        P(None, "dp"),
        P(None, "dp"),
        P(None, "dp"),
        P(None, ("dp", "seq"), None),
        P(None, ("dp", "seq"), None),
        P(None, ("dp", "seq")),
        P(None, ("dp", "seq")),
        P(),
        P(None, ("dp", "seq"), None),
        P(None, ("dp", "seq"), None),
        P(None, ("dp", "seq"), None),
        P(None, ("dp", "seq"), None),
        P(None, ("dp", "seq")),
        P(None, ("dp", "seq")),
        P(None, ("dp", "seq")),
        P(None, ("dp", "seq")),
        P(),
        P(),
        P(),
    )
    out_specs = (
        P(),
        P(),
        P(None, ("dp", "seq"), None),
        P(None, ("dp", "seq"), None),
        P(None, ("dp", "seq"), None),
        P(None, ("dp", "seq"), None),
        P(None, ("dp", "seq"), None),
        P(None, ("dp", "seq"), None),
        P(None, ("dp", "seq")),
        P(None, ("dp", "seq")),
        P(None, ("dp", "seq")),
        P(None, ("dp", "seq")),
        P(None, ("dp", "seq")),
        P(None, ("dp", "seq")),
        P(),
        P(),
        P(),
    )
    return jax.shard_map(shards, mesh=mesh, in_specs=in_specs, out_specs=out_specs, check_vma=False)
```

```python
from functools import partial
import math

import jax
import jax.numpy as jnp
from jax import lax
from jax.experimental import pallas as pl
from jax.experimental.pallas import tpu as pltpu
from jax.sharding import PartitionSpec as P

D = 1024
HEADS = 16
HEAD_DIM = 64
FF = 4096
CLASSES = 1000
FREQ = 256
PATCH = 16
GRID = 16
MICRO = 2
TOKENS_IMG = 256
MAIN = 4 * D + FF
MODS = 6 * D

clip_limit = 0.005
rate = 0.05
decay = 0.01

BOTH = ("dp", "seq")
END_CLASS = CLASSES + 1
END_T1 = END_CLASS + FREQ
END_T2 = END_T1 + D
END_PATCH = END_T2 + PATCH
END_FINAL = END_PATCH + 2 * D


def low(values):
    return values.astype(jnp.bfloat16)


def mm(left, right):
    return jnp.dot(left, right, preferred_element_type=jnp.float32)


def mm_tn(left, right):
    return lax.dot_general(
        left, right, (((0,), (0,)), ((), ())), preferred_element_type=jnp.float32
    )


def mm_nt(left, right):
    return lax.dot_general(
        left, right, (((1,), (1,)), ((), ())), preferred_element_type=jnp.float32
    )


def positions():
    quarter = D // 4
    omegas = 1.0 / 10000.0 ** (jnp.arange(quarter, dtype=jnp.float32) / quarter)
    angles = jnp.arange(GRID, dtype=jnp.int32).astype(jnp.float32)[:, None] * omegas[None, :]
    waves = jnp.concatenate([jnp.sin(angles), jnp.cos(angles)], axis=1)
    whole = (GRID, GRID, 2 * quarter)
    across = jnp.broadcast_to(waves[:, None], whole)
    along = jnp.broadcast_to(waves[None], whole)
    return jnp.concatenate([across, along], axis=2).reshape(TOKENS_IMG, D)


def time_features(time_steps):
    half_freq = FREQ // 2
    rates = jnp.exp(-math.log(10000.0) * jnp.arange(half_freq, dtype=jnp.float32) / half_freq)
    angles = time_steps.astype(jnp.float32)[:, None] * rates[None, :]
    return jnp.concatenate([jnp.cos(angles), jnp.sin(angles)], axis=1)


def signal_levels(time_steps):
    angles = (time_steps.astype(jnp.float32) / 1000.0 + 0.008) / 1.008 * (math.pi / 2.0)
    levels = jnp.cos(angles) ** 2
    return (jnp.sqrt(levels), jnp.sqrt(1.0 - levels))


def norm_stats(values):
    centred = values - jnp.mean(values, axis=-1, keepdims=True)
    inverse = lax.rsqrt(jnp.mean(centred * centred, axis=-1, keepdims=True) + 1e-06)
    return (centred * inverse, inverse)


def norm_back(grad, unit, inverse, scale):
    grad_unit = grad * (1.0 + scale)
    mean_one = jnp.mean(grad_unit, axis=-1, keepdims=True)
    mean_two = jnp.mean(grad_unit * unit, axis=-1, keepdims=True)
    grad_values = inverse * (grad_unit - mean_one - unit * mean_two)
    return (
        grad_values,
        jnp.sum(grad, axis=0, keepdims=True),
        jnp.sum(grad * unit, axis=0, keepdims=True),
    )


GELU_A = math.sqrt(2.0 / math.pi)
GELU_B = 0.044715


def gelu_both(values):
    squared = values * values
    bent = jnp.tanh(GELU_A * (values + GELU_B * squared * values))
    out = 0.5 * values * (1.0 + bent)
    slope = 0.5 * (1.0 + bent) + 0.5 * values * (1.0 - bent * bent) * (
        GELU_A * (1.0 + 3.0 * GELU_B * squared)
    )
    return (out, slope)


def silu_slope(values):
    sig = jax.nn.sigmoid(values)
    return sig * (1.0 + values * (1.0 - sig))


def heads_of(values):
    return values.reshape(values.shape[0], HEADS, HEAD_DIM)


def adam(weight, grad, first_m, second_m, factor, step_count):
    clipped = grad * factor
    first_new = 0.9 * first_m + 0.1 * clipped
    second_new = 0.999 * second_m + 0.001 * clipped * clipped
    first_hat = first_new / (1.0 - 0.9**step_count)
    second_hat = second_new / (1.0 - 0.999**step_count)
    updated = weight - rate * (first_hat / (jnp.sqrt(second_hat) + 1e-08) + decay * weight)
    return (updated, first_new, second_new)


ID_TYPE = pl.DeviceIdType.MESH
LINE = 4


def route():
    me, core = lax.axis_index("dp"), lax.axis_index("seq")
    place, line = me // LINE, me % LINE
    step_x, step_y = 1 - 2 * (line % 2), 2 - 4 * (line // 2)
    near = line + (1 - core) * step_y + core * step_x
    far = line + (1 - core) * step_x + core * step_y
    return core, place, line, near, far, line + step_x + step_y


def transfer(source, target, send_sem, recv_sem, device):
    return pltpu.make_async_remote_copy(
        src_ref=source,
        dst_ref=target,
        send_sem=send_sem,
        recv_sem=recv_sem,
        device_id=device,
        device_id_type=ID_TYPE,
    )


def packed(block):
    groups = [block[..., r : r + 8, :] for r in range(0, 32, 8)]
    return jnp.concatenate(groups, axis=-1)


def unpacked(tiles):
    groups = [tiles[..., c : c + 32] for c in range(0, 128, 32)]
    return jnp.concatenate(groups, axis=-2)


class Exchange:
    def __init__(self, n_dev, send_sem, recv_sem):
        self.n_dev, self.send_sem, self.recv_sem = n_dev, send_sem, recv_sem
        self.me = 2 * lax.axis_index("dp") + lax.axis_index("seq")
        self.started = []

    def greet(self):
        barrier = pltpu.get_barrier_semaphore()
        for k in range(1, self.n_dev):
            other = (self.me + k) % self.n_dev
            pl.semaphore_signal(
                barrier, inc=1, device_id=(other // 2, other % 2), device_id_type=ID_TYPE
            )
        pl.semaphore_wait(barrier, self.n_dev - 1)

    def post(self, row, source, out, each=False):
        sems = (self.send_sem.at[row], self.recv_sem.at[row])
        for k in range(1, self.n_dev):
            other = (self.me + k) % self.n_dev
            block = source.at[other] if each else source
            transfer(block, out.at[self.me], *sems, (other // 2, other % 2)).start()
        out[self.me] = source[self.me] if each else source[...]
        self.started.append((row, out))

    def all_but_one(self, row, out):
        some = out.at[pl.ds(0, self.n_dev - 1)]
        other = (self.me + 1) % self.n_dev
        return transfer(
            some, some, self.send_sem.at[row], self.recv_sem.at[row], (other // 2, other % 2)
        )

    def collect(self, row, out):
        self.all_but_one(row, out).wait_recv()

    def finish(self):
        for row, out in self.started:
            self.all_but_one(row, out).wait_send()


def gather_kernel(pieces, n_dev, *refs):
    wide_in, narrow_in, small, row, class_t, t1_t, t2_t, fs_t, fc_t, bias_t = refs[:10]
    refs = refs[10:]
    wholes, refs = refs[:2], refs[2:]
    small_all, rows_all, time_one, time_all, condition, cond_all, mods_came, final_came, ada = refs[:9]
    main_low, narrow_low, *refs = refs[9:]
    shards = (main_low, narrow_low)
    time_mine, cond_mine, time_came, cond_came, mods_wide, mods_mine, final_mine = refs[:7]
    send_sem, line_sem, near_sem, far_sem, core_sem, own_sem, swap_send, swap_recv = refs[7:]
    swaps = Exchange(n_dev, swap_send, swap_recv)
    core, place, line, near, far, both = route()
    to_next = (LINE * ((place + 1) % LINE) + line, core)
    to_near, to_far = (LINE * place + near, core), (LINE * place + far, core)
    to_core = (LINE * place + line, 1 - core)

    places = [(place + LINE - j) % LINE for j in range(LINE)]

    def block(piece, j, at, of=None):
        which, cut = pieces[piece]
        return wholes[which].at[(places[j], at, core if of is None else of, *cut)]

    def own_block(piece):
        which, cut = pieces[piece]
        return shards[which].at[cut]

    def own(piece):
        return pltpu.make_async_copy(own_block(piece), block(piece, 0, line), own_sem.at[piece])

    def hop(piece, j, at, stage, source=None):
        which = pieces[piece][0]
        target = block(piece, j, at)
        if stage == 3:
            arrived = core_sem.at[which]
        elif stage == 2:
            arrived = far_sem.at[piece, j if at is line or at is far else LINE + j]
        else:
            arrived = (line_sem, near_sem)[stage].at[piece, j]
        return transfer(
            target if source is None else source,
            target,
            send_sem.at[which, stage],
            arrived,
            (to_next, to_near, to_far, to_core)[stage],
        )

    def start_line(piece):
        which, cut = pieces[piece]
        shards[which][cut] = low((wide_in, narrow_in)[which][cut])
        hop(piece, 0, line, 0, own_block(piece)).start()
        own(piece).start()

    def start_others(piece):
        for stage in (1, 2, 3):
            hop(piece, 0, line, stage, own_block(piece)).start()

    def from_line(j, piece):
        target = block(piece, j, line)
        transfer(target, target, send_sem.at[pieces[piece][0], 0], line_sem.at[piece, j - 1], to_next).wait_recv()
        for stage in range(0 if j + 1 < LINE else 1, 4):
            hop(piece, j, line, stage).start()

    def from_near(j, piece):
        hop(piece, j, near, 1).wait_recv()
        hop(piece, j, near, 2).start()
        hop(piece, j, near, 3).start()

    def from_far(j, piece):
        hop(piece, j, far, 2).wait_recv()
        hop(piece, j, far, 3).start()

    def from_both(j, piece):
        hop(piece, j, both, 2).wait_recv()
        hop(piece, j, both, 3).start()

    def columns(which):
        return bias_t[:, which : which + 1]

    def time_step():
        for start in range(0, MODS, D):
            ada[:, start : start + D] = low(wide_in[:, MAIN + start : MAIN + start + D])
        swaps.collect(0, rows_all)
        freqs = jnp.concatenate([rows_all[:, 1, :], rows_all[:, 2, :]], axis=1)
        time_one[...] = mm_nt(t1_t[...], low(freqs)) + columns(15)
        time_mine[...] = packed(low(jax.nn.silu(time_one[...])).astype(jnp.float32))
        swaps.post(1, time_mine, time_came)

    def cond_step():
        labels = rows_all[:, 0, :]
        lanes = lax.broadcasted_iota(jnp.int32, labels.shape, 1).astype(jnp.float32)
        chosen = [
            jnp.where(labels == lanes + float(start), 1.0, 0.0)
            for start in range(0, class_t.shape[1], labels.shape[1])
        ]
        swaps.collect(1, time_came)
        time_all[...] = low(unpacked(time_came[...]))
        condition[...] = (
            mm(t2_t[...], time_all[...].reshape(D, n_dev))
            + columns(16)
            + mm_nt(class_t[...], low(jnp.concatenate(chosen, axis=1)))
        )
        act = low(jax.nn.silu(condition[...]))
        cond_mine[...] = packed(act.astype(jnp.float32))
        swaps.post(2, cond_mine, cond_came)
        for start in range(0, MODS, D):
            some = mm_tn(act, ada[:, start : start + D])
            for at in range(0, D, 128):
                mods_wide[:, (start + at) // 128, :] = some[:, at : at + 128]
        mods_mine[...] = low(mods_wide[...])
        swaps.post(3, mods_mine, mods_came, each=True)

    def final_step():
        swaps.collect(2, cond_came)
        cond_all[...] = low(unpacked(cond_came[...]))
        acts = cond_all[...].reshape(D, n_dev)
        both_t = [mm(fs_t[...], acts) + columns(17), mm(fc_t[...], acts) + columns(18)]
        final_mine[:, 0, :] = jnp.concatenate(both_t, axis=0).T
        swaps.post(4, final_mine, final_came, each=True)

    total = len(pieces)
    plan = [(AG_EXTRAS[0], time_step), (AG_EXTRAS[1], cond_step), (AG_EXTRAS[2], final_step)]
    for piece in range(total):
        share = piece * 12.0 / total
        plan.append((AG_START[0] * share + AG_START[1], partial(start_line, piece)))
        plan.append((AG_OTHERS[0] * share + AG_OTHERS[1], partial(start_others, piece)))
        for step, (slope, first) in zip((from_line, from_near, from_far, from_both), AG_PLAN):
            for j in range(0 if step is not from_line else 1, LINE):
                plan.append((slope * share + first + AG_HOP * max(j, 1), partial(step, j, piece)))
    swaps.greet()
    swaps.post(0, row, rows_all)
    swaps.post(5, small, small_all)
    for _, step in sorted(plan, key=lambda planned: planned[0]):
        step()
    for exchange_row, out in ((3, mods_came), (4, final_came), (5, small_all)):
        swaps.collect(exchange_row, out)
    swaps.finish()
    for piece in range(total):
        own(piece).wait()
    for which, whole in enumerate(wholes):
        theirs = whole.at[:, :, 1 - core]
        transfer(theirs, theirs, send_sem.at[which, 3], core_sem.at[which], to_core).wait_recv()
        spans = (
            whole.at[pl.ds(0, LINE - 1), 0, 0],
            whole.at[:, 0, 0],
            whole.at[:, pl.ds(0, 2), 0],
            whole.at[:, :, 0],
        )
        for stage, span in enumerate(spans):
            transfer(span, span, send_sem.at[which, stage], core_sem.at[which], to_core).wait_send()


def gather_and_condition(inputs, n_dev, pieces):
    part = D // n_dev
    shards = [(part, MAIN), inputs[1].shape]
    vmem, anywhere = pl.BlockSpec(memory_space=pltpu.VMEM), pl.BlockSpec(memory_space=pl.ANY)
    wide, narrow = jnp.float32, jnp.bfloat16
    out_shape = [jax.ShapeDtypeStruct((LINE, LINE, 2, *s), narrow) for s in shards]
    out_shape += [
        jax.ShapeDtypeStruct((n_dev, *inputs[2].shape), narrow),
        jax.ShapeDtypeStruct((n_dev, *inputs[3].shape), wide),
        jax.ShapeDtypeStruct((part, n_dev), wide),
        jax.ShapeDtypeStruct((n_dev, part, n_dev), narrow),
        jax.ShapeDtypeStruct((part, n_dev), wide),
        jax.ShapeDtypeStruct((n_dev, part, n_dev), narrow),
        jax.ShapeDtypeStruct((n_dev, MODS // 128, 128), narrow),
        jax.ShapeDtypeStruct((n_dev, 1, 2 * part), wide),
        jax.ShapeDtypeStruct((part, MODS), narrow),
    ]
    return pl.pallas_call(
        partial(gather_kernel, pieces, n_dev),
        out_shape=out_shape,
        in_specs=[vmem] * len(inputs),
        out_specs=[anywhere] * 2 + [vmem] * 9,
        scratch_shapes=[
            *(pltpu.VMEM(s, narrow) for s in shards),
            pltpu.VMEM((8, 128), wide),
            pltpu.VMEM((8, 128), wide),
            pltpu.VMEM((n_dev, 8, 128), wide),
            pltpu.VMEM((n_dev, 8, 128), wide),
            pltpu.VMEM((n_dev, MODS // 128, 128), wide),
            pltpu.VMEM((n_dev, MODS // 128, 128), narrow),
            pltpu.VMEM((n_dev, 1, 2 * part), wide),
            pltpu.SemaphoreType.DMA((2, 4)),
            pltpu.SemaphoreType.DMA((len(pieces), LINE - 1)),
            pltpu.SemaphoreType.DMA((len(pieces), LINE)),
            pltpu.SemaphoreType.DMA((len(pieces), 2 * LINE)),
            pltpu.SemaphoreType.DMA((2,)),
            pltpu.SemaphoreType.DMA((len(pieces),)),
            pltpu.SemaphoreType.DMA((6,)),
            pltpu.SemaphoreType.DMA((6,)),
        ],
        compiler_params=pltpu.CompilerParams(
            collective_id=0, has_side_effects=True, vmem_limit_bytes=58 * 2**20
        ),
    )(*inputs)


def scatter_kernel(pieces, count, n_dev, *refs):
    parts, refs = refs[:count], refs[count:]
    sum_rows, refs = refs[:8], refs[8:]
    inputs, refs = refs[:11], refs[11:]
    mods_low, sums_mine, ada, fs_t, fc_t, t2_t, condition, time_one, cond_all, time_all, rows_all = inputs
    (out_narrow, out_wide, g_class, g_t1, g_t2, g_fs, g_fc), refs = refs[:7], refs[7:]
    small_sum, g_bias, totals = refs[:3]
    mods_all, small_mine, small_all, squares_mine, sums_all, squares_all, small_part = refs[3:10]
    cond_part, cond_came, time_part, time_came, mods_wide, mods_rows, low_cond = refs[10:17]
    refs = refs[17:]
    held, from_core, from_far, from_near, from_line = (
        refs[i * count : (1 + i) * count] for i in range(5)
    )
    send_sem, core_sem, far_sem, near_sem, line_sem, load_sem, swap_send, swap_recv = refs[5 * count :]
    swaps = Exchange(n_dev, swap_send, swap_recv)
    core, place, line, near, far, both = route()
    lanes = (line, near, far, both)
    lanes_there = (line, far, near, both)
    to_near, to_far = (LINE * place + near, core), (LINE * place + far, core)
    to_core = (LINE * place + line, 1 - core)
    order = (3, 2, 1, 0)
    out_at = (0, 4 * D, 3 * D, 0)

    def view(refs_of, piece, *at):
        which, cut = pieces[piece]
        return refs_of[which].at[(*at, *(slice(None) for _ in range(2 - len(at))), *cut)]

    def sent(piece, stage):
        return send_sem.at[pieces[piece][0], stage]

    def over_core(piece, lane):
        which, cut = pieces[piece]
        source = parts[which].at[(slice(None), lanes_there[lane], 1 - core, *cut)]
        target = view(from_core, piece, lane)
        return transfer(source, target, sent(piece, 0), core_sem.at[piece, lane], to_core)

    def load(piece, lane):
        which, cut = pieces[piece]
        source = parts[which].at[(slice(None), lanes[lane], core, *cut)]
        return pltpu.make_async_copy(source, view(held, piece, lane), load_sem.at[piece, lane])

    def over_far(piece):
        which, cut = pieces[piece]
        source = held[which].at[(pl.ds(2, 2), slice(None), *cut)]
        target = from_far[which].at[(pl.ds(0, 2), slice(None), *cut)]
        return transfer(source, target, sent(piece, 1), far_sem.at[piece], to_far)

    def over_near(piece):
        which, cut = pieces[piece]
        source, target = view(held, piece, 1), from_near[which].at[(slice(None), *cut)]
        return transfer(source, target, sent(piece, 2), near_sem.at[piece], to_near)

    def over_line(piece, k):
        which, cut = pieces[piece]
        there = (place + k) % LINE
        source, target = view(held, piece, 0, there), from_line[which].at[(k - 1, *cut)]
        device = (LINE * there + line, core)
        return transfer(source, target, sent(piece, 3), line_sem.at[piece, k - 1], device)

    def add(piece, lane, others_of, *at):
        which, cut = pieces[piece]
        mine, other = held[which], others_of[which]

        def one(i, carry):
            total = mine[(lane, i, *cut)].astype(jnp.float32) + other[(*at, i, *cut)].astype(
                jnp.float32
            )
            mine[(lane, i, *cut)] = total.astype(jnp.bfloat16)
            return carry

        lax.fori_loop(0, LINE, one, 0)

    def begin(piece):
        for lane in order:
            over_core(piece, lane).start()
            load(piece, lane).start()

    def by_core(piece):
        for lane in order:
            load(piece, lane).wait()
            over_core(piece, lane).wait_recv()
            add(piece, lane, from_core, lane)
            if lane == 2:
                over_far(piece).start()

    def by_far(piece):
        over_far(piece).wait_recv()
        add(piece, 1, from_far, 1)
        over_near(piece).start()
        add(piece, 0, from_far, 0)

    def by_near(piece):
        over_near(piece).wait_recv()
        add(piece, 0, from_near)
        for k in range(1, LINE):
            over_line(piece, k).start()

    squares, part = [], D // n_dev

    def squared(values):
        squares.append(jnp.sum(values * values))
        return values

    def by_line(piece):
        which, cut = pieces[piece]
        total = held[which][(0, place, *cut)].astype(jnp.float32)
        for k in range(1, LINE):
            over_line(piece, k).wait_recv()
            total = total + from_line[which][(k - 1, *cut)].astype(jnp.float32)
        squared(total)
        if which == 0:
            out_narrow[cut] = total
        else:
            first = out_at[which] + cut[1].start
            out_wide[:, first : first + total.shape[1]] = total

    def contract_first(left, right, right_dim):
        return lax.dot_general(
            left, right, (((0,), (right_dim,)), ((), ())), preferred_element_type=jnp.float32
        )

    def final_step():
        swaps.collect(2, small_all)
        sums = jnp.sum(small_all[...], axis=0)
        rows = jnp.concatenate([sums[:, c : c + part] for c in (0, 32, 64)], axis=0)
        small_sum[...] = squared(rows)
        by_image = squared(sums[:8, 96:])
        g_bias[:8] = rows[:8]
        g_bias[8:14] = by_image[:6]
        g_bias[14:15] = rows[8:9]
        g_bias[17:19] = by_image[6:]
        shift, scale = low(small_all[:, 6, 96:]), low(small_all[:, 7, 96:])
        back = contract_first(fs_t[...], shift, 1) + contract_first(fc_t[...], scale, 1)
        cond_part[...] = packed(back.reshape(n_dev, part, n_dev))
        swaps.post(4, cond_part, cond_came, each=True)
        acts = cond_all[...].reshape(D, n_dev)
        g_fs[...] = squared(contract_first(shift, acts, 1))
        g_fc[...] = squared(contract_first(scale, acts, 1))

    def cond_step():
        swaps.collect(0, mods_all)
        mods_wide[...] = mods_all[...].astype(jnp.float32)
        for i in range(6):
            mods_rows[:, D * i : D * (i + 1)] = low(mods_wide[:, i, :])
        back = mm_nt(ada[...], mods_rows[...])
        swaps.collect(4, cond_came)
        back = back + unpacked(jnp.sum(cond_came[...], axis=0))
        low_back = low(back * silu_slope(condition[...]))
        low_cond[...] = low_back
        time_part[...] = packed(contract_first(t2_t[...], low_back, 0).reshape(n_dev, part, n_dev))
        swaps.post(5, time_part, time_came, each=True)
        acts = cond_all[swaps.me]
        for start in range(0, MODS, D):
            some = squared(mm(acts, mods_rows[:, start : start + D]))
            out_wide[:, MAIN + start : MAIN + start + D] = some

    def time_step():
        low_back = low_cond[...]
        ones = jnp.ones((8, n_dev), jnp.bfloat16)
        g_bias[16:17] = squared(mm_nt(ones, low_back)[:1])
        labels = rows_all[:, 0, :]
        lanes = lax.broadcasted_iota(jnp.int32, labels.shape, 1).astype(jnp.float32)
        for start in range(0, g_class.shape[1], labels.shape[1]):
            chosen = low(jnp.where(labels == lanes + float(start), 1.0, 0.0))
            g_class[:, start : start + labels.shape[1]] = squared(mm(low_back, chosen))
        g_t2[...] = squared(mm_nt(low_back, time_all[...].reshape(D, n_dev)))
        swaps.collect(3, sums_all)
        swaps.collect(5, time_came)
        low_time = low(unpacked(jnp.sum(time_came[...], axis=0)) * silu_slope(time_one[...]))
        g_bias[15:16] = squared(mm_nt(ones, low_time)[:1])
        freqs = jnp.concatenate([rows_all[:, 1, :], rows_all[:, 2, :]], axis=1)
        g_t1[...] = squared(mm(low_time, low(freqs)))

    total = len(pieces)
    plan = [(RS_EXTRAS[0], final_step), (RS_EXTRAS[1], cond_step), (RS_EXTRAS[2], time_step)]
    for piece in range(total):
        share, when = piece * 12.0 / total, -100.0
        plan.append((RS_BEGIN[0] * share + RS_BEGIN[1], partial(begin, piece)))
        for (slope, first), step in zip(RS_PLAN, (by_core, by_far, by_near, by_line)):
            when = max(when + 0.1, slope * share + first)
            plan.append((when, partial(step, piece)))
    packed_sum, branch_sum, up_sum, down_sum, embed_sum, patch, out_rows, last_rows = sum_rows
    small_part[0:1] = packed_sum[:, :D]
    small_part[1:2] = packed_sum[:, 2 * D :]
    small_part[2:3] = branch_sum[...]
    for i in range(4):
        small_part[3 + i : 4 + i] = up_sum[:, D * i : D * (i + 1)]
    small_part[7:8] = down_sum[...]
    small_part[8:9] = embed_sum[...]
    small_part[9:25] = patch[...]
    small_part[25:41] = out_rows[...]
    small_part[41:48] = last_rows[...]
    small_part[48:56] = mods_low[...].astype(jnp.float32)
    small_part[56:64] = jnp.zeros((8, D), jnp.float32)
    for other in range(n_dev):
        own = slice(other * part, (other + 1) * part)
        groups = [small_part[r : r + 16, own] for r in (0, 16, 32, 48)]
        small_mine[other] = jnp.concatenate(groups, axis=1)
    swaps.greet()
    swaps.post(2, small_mine, small_all, each=True)
    swaps.post(0, mods_low, mods_all)
    swaps.post(3, sums_mine, sums_all)
    for _, step in sorted(plan, key=lambda planned: planned[0]):
        step()
    squares_mine[...] = jnp.broadcast_to(sum(squares), squares_mine.shape)
    swaps.post(6, squares_mine, squares_all)
    sums = jnp.sum(sums_all[...], axis=0)
    lanes = lax.broadcasted_iota(jnp.int32, sums.shape, 1)
    head_sums = jnp.where((lanes >= 1) & (lanes <= PATCH), sums, 0.0)
    swaps.collect(6, squares_all)
    all_squares = jnp.sum(squares_all[...], axis=0) + jnp.sum(head_sums * head_sums)
    totals[0:1] = sums
    totals[1:2] = jnp.sqrt(all_squares)
    swaps.finish()
    for which in range(count):
        for stage, span in enumerate((from_core, from_far, from_near, from_line)):
            transfer(
                span[which], span[which], send_sem.at[which, stage], core_sem.at[0, 0], to_core
            ).wait_send()


def scatter_and_condition(parts, inputs, n_dev, pieces):
    count, part = len(parts), D // n_dev
    shards = [p.shape[3:] for p in parts]
    vmem, anywhere = pl.BlockSpec(memory_space=pltpu.VMEM), pl.BlockSpec(memory_space=pl.ANY)
    wide, narrow = jnp.float32, jnp.bfloat16
    outs = [shards[0], (part, MAIN + MODS)]
    outs += [(part, D), (part, FREQ), (part, D), (part, D), (part, D)]
    outs += [(48, part), (19, part), (2, 128)]
    return pl.pallas_call(
        partial(scatter_kernel, pieces, count, n_dev),
        out_shape=[jax.ShapeDtypeStruct(s, wide) for s in outs],
        in_specs=[anywhere] * count + [vmem] * len(inputs),
        out_specs=[vmem] * len(outs),
        scratch_shapes=[
            pltpu.VMEM((n_dev, 8, D), narrow),
            pltpu.VMEM((n_dev, 16, 128), wide),
            pltpu.VMEM((n_dev, 16, 128), wide),
            pltpu.VMEM((1, 128), wide),
            pltpu.VMEM((n_dev, 1, 128), wide),
            pltpu.VMEM((n_dev, 1, 128), wide),
            pltpu.VMEM((64, D), wide),
            *(pltpu.VMEM((n_dev, 8, 128), wide) for _ in range(4)),
            pltpu.VMEM((n_dev, 8, D), wide),
            pltpu.VMEM((n_dev, MODS), narrow),
            pltpu.VMEM((part, n_dev), narrow),
            *(
                pltpu.VMEM((*blocks, *s), narrow)
                for blocks in ((4, LINE), (4, LINE), (2, LINE), (LINE,), (LINE - 1,))
                for s in shards
            ),
            pltpu.SemaphoreType.DMA((count, 4)),
            pltpu.SemaphoreType.DMA((len(pieces), 4)),
            pltpu.SemaphoreType.DMA((len(pieces),)),
            pltpu.SemaphoreType.DMA((len(pieces),)),
            pltpu.SemaphoreType.DMA((len(pieces), LINE - 1)),
            pltpu.SemaphoreType.DMA((len(pieces), 4)),
            pltpu.SemaphoreType.DMA((7,)),
            pltpu.SemaphoreType.DMA((7,)),
        ],
        compiler_params=pltpu.CompilerParams(
            collective_id=1, has_side_effects=True, vmem_limit_bytes=58 * 2**20
        ),
    )(*parts, *inputs)


AG_START = (4.0, -9.0)
AG_OTHERS = (4.0, -8.5)
AG_HOP = 4.25
AG_PLAN = ((4.0, 0.0), (5.0, 2.0), (5.0, 4.0), (8.5, 8.0))
AG_EXTRAS = (10.0, 25.0, 45.0)
RS_BEGIN = (8.5, -12.0)
RS_PLAN = ((8.5, 0.0), (8.5, 6.5), (8.5, 13.0), (8.5, 19.5))
RS_EXTRAS = (12.0, 30.0, 60.0)
AG_CUT = 1024
RS_CUT = 512


def tiled(n_dev):
    return n_dev == 8 * LINE and (D // n_dev) % 16 == 0


def column_cuts(which, columns, step):
    return [(which, (slice(None), slice(c, c + step))) for c in range(0, columns, step)]


def row_cuts(which, rows, step):
    return [(which, (slice(r, r + step), slice(None))) for r in range(0, rows, step)]


def first_part(wide, narrow, small, row, table_t, bias_t, n_dev):
    class_t, t1_t, t2_t, fs_t, fc_t = table_t
    if tiled(n_dev):
        pieces = column_cuts(0, MAIN, AG_CUT) + row_cuts(1, FF // n_dev, AG_CUT // 32)
        inputs = [wide, narrow, small.reshape(-1, 128), row, class_t, t1_t, t2_t, fs_t, fc_t, bias_t]
        out = gather_and_condition(inputs, n_dev, tuple(pieces))
        main_all, narrow_all, *rest = out
        return [main_all.reshape(D, MAIN), narrow_all.reshape(FF, D), *rest]
    main_all = lax.all_gather(low(wide[:, :MAIN]), BOTH, axis=0, tiled=True)
    narrow_all = lax.all_gather(low(narrow), BOTH, axis=0, tiled=True)
    ada = low(wide[:, MAIN:])
    small_all = lax.all_gather(small, BOTH)
    rows_all = lax.all_gather(row, BOTH)
    freqs = low(rows_all[:, 1:3].reshape(n_dev, FREQ))
    time_one = mm_nt(t1_t, freqs) + bias_t[:, 15:16]
    time_all = lax.all_gather(low(jax.nn.silu(time_one)), BOTH)
    classes = jnp.arange(class_t.shape[1], dtype=jnp.int32).astype(jnp.float32)
    choose = low(rows_all[:, 0, :1] == classes)
    condition = (
        mm(t2_t, time_all.reshape(D, n_dev)) + bias_t[:, 16:17] + mm_nt(class_t, choose)
    )
    cond_mine = low(jax.nn.silu(condition))
    cond_all = lax.all_gather(cond_mine, BOTH)
    mods_mine = low(mm_tn(cond_mine, ada)).reshape(n_dev, MODS // 128, 128)
    mods_came = lax.all_to_all(mods_mine, BOTH, 0, 0, tiled=True)
    acts = cond_all.reshape(D, n_dev)
    both_t = [mm(fs_t, acts) + bias_t[:, 17:18], mm(fc_t, acts) + bias_t[:, 18:19]]
    final_mine = jnp.concatenate(both_t, axis=0).T[:, None]
    final_came = lax.all_to_all(final_mine, BOTH, 0, 0, tiled=True)
    return [main_all, narrow_all, small_all, rows_all, time_one, time_all, condition, cond_all, mods_came, final_came, ada]


def last_part(parts, mods_row, sum_rows, sums_mine, ada, table_t, condition, time_one, cond_all, time_all, rows_all, n_dev):
    _, _, t2_t, fs_t, fc_t = table_t
    mods_low = low(mods_row)
    if tiled(n_dev):
        blocks = [p.reshape(LINE, LINE, 2, p.shape[0] // n_dev, p.shape[1]) for p in parts]
        pieces = row_cuts(0, FF // n_dev, RS_CUT // 32)
        for which in range(1, len(parts)):
            pieces += column_cuts(which, parts[which].shape[1], RS_CUT)
        inputs = [*sum_rows, mods_low, sums_mine, ada, fs_t, fc_t, t2_t, condition, time_one]
        inputs += [cond_all, time_all, rows_all]
        return scatter_and_condition(blocks, inputs, n_dev, tuple(pieces))
    part = D // n_dev
    shards = [
        lax.psum_scatter(p, BOTH, scatter_dimension=0, tiled=True).astype(jnp.float32) for p in parts
    ]

    def by_owner(rows):
        cut = jnp.transpose(rows.reshape(rows.shape[0], n_dev, part), (1, 0, 2))
        return lax.all_to_all(cut, BOTH, 0, 0, tiled=True)

    mods_all = lax.all_gather(mods_low, BOTH).reshape(n_dev, 8 * D)[:, :MODS]
    cut_all = by_owner(mods_low.astype(jnp.float32))
    sum_rows = [sum_rows[0][:, :D], sum_rows[0][:, 2 * D :], *sum_rows[1:]]
    small_part = jnp.concatenate([rows.reshape(-1, D) for rows in sum_rows], axis=0)
    small_sum = jnp.sum(by_owner(small_part), axis=0)
    sums = jnp.sum(lax.all_gather(sums_mine, BOTH), axis=0)
    shift, scale = low(cut_all[:, 6]), low(cut_all[:, 7])
    back = mm(shift, fs_t) + mm(scale, fc_t)
    back = lax.all_to_all(back.T.reshape(n_dev, part, n_dev), BOTH, 0, 0, tiled=True)
    back = jnp.sum(back, axis=0) + mm_nt(ada, mods_all)
    grad_cond = low(back * silu_slope(condition))
    back = mm_tn(t2_t, grad_cond).reshape(n_dev, part, n_dev)
    back = jnp.sum(lax.all_to_all(back, BOTH, 0, 0, tiled=True), axis=0)
    grad_time = low(back * silu_slope(time_one))
    acts = cond_all.reshape(D, n_dev)
    me_cond = lax.dynamic_index_in_dim(cond_all, lax.axis_index(BOTH), 0, keepdims=False)
    classes = jnp.arange(D, dtype=jnp.int32).astype(jnp.float32)
    grads = [
        shards[0],
        jnp.concatenate([shards[3], shards[2], shards[1], mm(me_cond, mods_all)], axis=1),
        mm(grad_cond, low(rows_all[:, 0, :1] == classes)),
        mm(grad_time, low(rows_all[:, 1:3].reshape(n_dev, FREQ))),
        mm_nt(grad_cond, time_all.reshape(D, n_dev)),
        mm(shift.T, acts.T),
        mm(scale.T, acts.T),
        small_sum,
    ]
    cut_sum = jnp.sum(cut_all, axis=0)
    row_of = lambda grad: jnp.sum(grad, axis=1, dtype=jnp.float32)[None]
    bias_rest = [cut_sum, row_of(grad_time), row_of(grad_cond)]
    squares = sum(jnp.sum(g * g) for g in grads + bias_rest)
    squares = jnp.sum(lax.all_gather(squares[None], BOTH)) + jnp.sum(jnp.square(sums[:, 1 : PATCH + 1]))
    g_bias = jnp.concatenate(
        [small_sum[:8], cut_sum[:6], small_sum[8:9], bias_rest[1], bias_rest[2], cut_sum[6:]], axis=0
    )
    return [*grads, g_bias, jnp.concatenate([sums, jnp.full_like(sums, jnp.sqrt(squares))], axis=0)]


def shards(
    latents,
    noises,
    labels,
    dropped,
    timesteps,
    layer_in,
    layer_out,
    cond_table,
    bias_rows,
    head_bias,
    layer_in_m,
    layer_in_v,
    layer_out_m,
    layer_out_v,
    cond_table_m,
    cond_table_v,
    bias_rows_m,
    bias_rows_v,
    head_bias_m,
    head_bias_v,
    adam_step,
):
    core = lax.axis_index("seq")
    chips = lax.axis_size("dp")
    n_dev = chips * lax.axis_size("seq")
    me = lax.axis_index("dp") * 2 + core
    norm_count = float(MICRO * chips * TOKENS_IMG * PATCH)
    part = layer_in.shape[1]

    pair = jnp.concatenate([latents[:, 0], noises[:, 0]], axis=2)
    other = lax.dynamic_index_in_dim(pair, 1 - core, 0, keepdims=False)
    mine = lax.dynamic_index_in_dim(pair, core, 0, keepdims=False)
    came = lax.ppermute(other, "seq", [(0, 1), (1, 0)])
    image = jnp.where(core == 0, jnp.concatenate([mine, came]), jnp.concatenate([came, mine]))
    latent, noise = image[:, :PATCH], image[:, PATCH:]

    my_label, my_drop, my_time = (
        jnp.where(core == 0, both[0], both[1]) for both in (labels, dropped, timesteps)
    )
    my_class = jnp.where(my_drop == 1, CLASSES, my_label).astype(jnp.float32)
    my_freqs = low(time_features(my_time)).astype(jnp.float32)
    row = jnp.concatenate(
        [jnp.broadcast_to(my_class[None], (1, 128)), my_freqs.reshape(2, 128), jnp.zeros((5, 128))]
    )

    table_t = low(cond_table.T)
    bias_low = low(bias_rows)
    bias_t = bias_low.astype(jnp.float32).T

    small = jnp.concatenate(
        [bias_low, table_t[:, END_T2:END_PATCH].T, table_t[:, END_FINAL:].T, jnp.zeros_like(bias_low[:1])],
        axis=0,
    )
    table_parts = (
        jnp.pad(table_t[:, :END_CLASS], ((0, 0), (0, D - END_CLASS))),
        table_t[:, END_CLASS:END_T1],
        table_t[:, END_T1:END_T2],
        table_t[:, END_PATCH : END_PATCH + D],
        table_t[:, END_PATCH + D : END_FINAL],
    )
    (
        main_all,
        narrow_all,
        small_all,
        rows_all,
        time_one,
        time_all,
        condition,
        cond_all,
        mods_came,
        final_came,
        ada_low,
    ) = first_part(layer_in[0], layer_out[0], small, row, table_parts, bias_t, n_dev)
    small_all = jnp.transpose(small_all.reshape(n_dev, 52, part), (1, 0, 2)).reshape(52, D)
    bias_all = small_all[:19].astype(jnp.float32)
    patch_w = small_all[19:35]
    out_w = small_all[35:51]
    mods = (
        jnp.sum(mods_came.astype(jnp.float32), axis=0).reshape(1, MODS)
        + bias_all[8:14].reshape(1, MODS)
    )
    f_shift = final_came[:, 0, :part].reshape(1, D)
    f_scale = final_came[:, 0, part:].reshape(1, D)
    shift_a, scale_a, gate_a, shift_b, scale_b, gate_b = jnp.split(mods, 6, axis=1)

    keep_level, spread = signal_levels(my_time)
    noisy = low(keep_level[:, None] * latent + spread[:, None] * noise)
    hidden = mm(noisy, patch_w) + bias_all[14] + positions()
    unit_a, inv_a = norm_stats(hidden)
    normed_a = low(unit_a * (1.0 + scale_a) + shift_a)
    bias_qkv = jnp.concatenate([bias_all[0], jnp.zeros((D,), jnp.float32), bias_all[1]])
    packed = low(mm(normed_a, main_all[:, : 3 * D]) + bias_qkv)
    queries, keys, values = (heads_of(packed[:, i * D : (i + 1) * D]) for i in range(3))
    head_scale = 1.0 / math.sqrt(HEAD_DIM)
    scores = (
        jnp.einsum("shd,khd->hsk", queries, keys, preferred_element_type=jnp.float32) * head_scale
    )
    expd = jnp.exp(scores - jnp.max(scores, axis=-1, keepdims=True))
    probs = expd / jnp.sum(expd, axis=-1, keepdims=True)
    probs_low = low(probs)
    attended = jnp.einsum("hsk,khd->shd", probs_low, values, preferred_element_type=jnp.float32)
    attended = low(attended.reshape(TOKENS_IMG, D))
    branch = mm(attended, main_all[:, 3 * D : 4 * D]) + bias_all[2]
    middle = hidden + gate_a * branch
    unit_b, inv_b = norm_stats(middle)
    normed_b = low(unit_b * (1.0 + scale_b) + shift_b)
    upward = mm(normed_b, main_all[:, 4 * D :]) + bias_all[3:7].reshape(FF)
    activated, slope = gelu_both(upward)
    activated = low(activated)
    downward = mm(activated, narrow_all) + bias_all[7]
    last = middle + gate_b * downward
    unit_f, inv_f = norm_stats(last)
    normed_f = low(unit_f * (1.0 + f_scale) + f_shift)
    predicted = mm_nt(normed_f, out_w) + head_bias

    differ = predicted - noise
    loss_part = jnp.sum(differ * differ) / norm_count
    grad_pred = low(2.0 * differ / norm_count)
    head_part = jnp.sum(grad_pred, axis=0, dtype=jnp.float32)
    grad_out_w = mm_tn(grad_pred, normed_f)
    grad_last, g_fshift, g_fscale = norm_back(mm(grad_pred, out_w), unit_f, inv_f, f_scale)
    g_gate_b = jnp.sum(grad_last * downward, axis=0, keepdims=True)
    grad_down = low(gate_b * grad_last)
    grad_narrow = low(mm_tn(activated, grad_down))
    grad_up = low(slope * mm_nt(grad_down, narrow_all))
    grad_fc1 = low(mm_tn(normed_b, grad_up))
    grad_mid, g_shift_b, g_scale_b = norm_back(
        mm_nt(grad_up, main_all[:, 4 * D :]), unit_b, inv_b, scale_b
    )
    grad_middle = grad_last + grad_mid
    g_gate_a = jnp.sum(grad_middle * branch, axis=0, keepdims=True)
    grad_branch = low(gate_a * grad_middle)
    grad_proj = low(mm_tn(attended, grad_branch))
    grad_att = heads_of(low(mm_nt(grad_branch, main_all[:, 3 * D : 4 * D])))
    grad_probs = jnp.einsum("shd,khd->hsk", grad_att, values, preferred_element_type=jnp.float32)
    grad_values = jnp.einsum("hsk,shd->khd", probs_low, grad_att, preferred_element_type=jnp.float32)
    grad_scores = low(
        probs * (grad_probs - jnp.sum(grad_probs * probs, axis=-1, keepdims=True))
    )
    grad_queries = (
        jnp.einsum("hsk,khd->shd", grad_scores, keys, preferred_element_type=jnp.float32)
        * head_scale
    )
    grad_keys = (
        jnp.einsum("hsk,shd->khd", grad_scores, queries, preferred_element_type=jnp.float32)
        * head_scale
    )
    grad_packed = low(
        jnp.concatenate(
            [g.reshape(TOKENS_IMG, D) for g in (grad_queries, grad_keys, grad_values)], axis=1
        )
    )
    grad_qkv = low(mm_tn(normed_a, grad_packed))
    grad_hid, g_shift_a, g_scale_a = norm_back(
        mm_nt(grad_packed, main_all[:, : 3 * D]), unit_a, inv_a, scale_a
    )
    grad_embed = low(grad_middle + grad_hid)
    grad_patch = mm_tn(noisy, grad_embed)

    row_sums = lambda values: jnp.sum(values.astype(jnp.float32), axis=0, keepdims=True)
    sum_rows = [
        row_sums(grad_packed),
        row_sums(grad_branch),
        row_sums(grad_up),
        row_sums(grad_down),
        row_sums(grad_embed),
        grad_patch,
        grad_out_w,
        jnp.zeros((7, D)),
    ]
    sums_mine = jnp.pad(jnp.concatenate([loss_part[None], head_part]), (0, 111))[None]
    mods_row = low(
        jnp.concatenate(
            [g_shift_a, g_scale_a, g_gate_a, g_shift_b, g_scale_b, g_gate_b, g_fshift, g_fscale],
            axis=0,
        )
    )
    (
        grad_narrow,
        grad_wide,
        grad_class,
        grad_t1,
        grad_t2,
        grad_fs,
        grad_fc,
        small_sum,
        grad_bias,
        totals,
    ) = last_part(
        [grad_narrow, grad_fc1, grad_proj, grad_qkv],
        mods_row,
        sum_rows,
        sums_mine,
        ada_low,
        table_parts,
        condition,
        time_one,
        cond_all,
        time_all,
        rows_all,
        n_dev,
    )
    loss_total, head_total = totals[0, 0], totals[0, 1 : PATCH + 1]
    grad_table = jnp.concatenate(
        [
            grad_class[:, :END_CLASS],
            grad_t1,
            grad_t2,
            small_sum[9:25].T,
            grad_fs,
            grad_fc,
            small_sum[25:41].T,
        ],
        axis=1,
    ).T
    grad_wide, grad_narrow = grad_wide[None], grad_narrow[None]
    norm = totals[1, 0]
    factor = jnp.minimum(1.0, clip_limit / (norm + 1e-06))
    step_count = adam_step[0].astype(jnp.float32)
    results = [loss_total, norm]
    results.extend(adam(layer_in, grad_wide, layer_in_m, layer_in_v, factor, step_count))
    results.extend(adam(layer_out, grad_narrow, layer_out_m, layer_out_v, factor, step_count))
    results.extend(adam(cond_table, grad_table, cond_table_m, cond_table_v, factor, step_count))
    results.extend(adam(bias_rows, grad_bias, bias_rows_m, bias_rows_v, factor, step_count))
    results.extend(adam(head_bias, head_total, head_bias_m, head_bias_v, factor, step_count))
    return tuple(results)


def solution(mesh):
    in_specs = (
        P(None, "dp", "seq", None),
        P(None, "dp", "seq", None),
        P(None, "dp"),
        P(None, "dp"),
        P(None, "dp"),
        P(None, ("dp", "seq"), None),
        P(None, ("dp", "seq"), None),
        P(None, ("dp", "seq")),
        P(None, ("dp", "seq")),
        P(),
        P(None, ("dp", "seq"), None),
        P(None, ("dp", "seq"), None),
        P(None, ("dp", "seq"), None),
        P(None, ("dp", "seq"), None),
        P(None, ("dp", "seq")),
        P(None, ("dp", "seq")),
        P(None, ("dp", "seq")),
        P(None, ("dp", "seq")),
        P(),
        P(),
        P(),
    )
    out_specs = (
        P(),
        P(),
        P(None, ("dp", "seq"), None),
        P(None, ("dp", "seq"), None),
        P(None, ("dp", "seq"), None),
        P(None, ("dp", "seq"), None),
        P(None, ("dp", "seq"), None),
        P(None, ("dp", "seq"), None),
        P(None, ("dp", "seq")),
        P(None, ("dp", "seq")),
        P(None, ("dp", "seq")),
        P(None, ("dp", "seq")),
        P(None, ("dp", "seq")),
        P(None, ("dp", "seq")),
        P(),
        P(),
        P(),
    )
    return jax.shard_map(shards, mesh=mesh, in_specs=in_specs, out_specs=out_specs, check_vma=False)
```

```python
from functools import partial
import math

import jax
import jax.numpy as jnp
from jax import lax
from jax.experimental import pallas as pl
from jax.experimental.pallas import tpu as pltpu
from jax.sharding import PartitionSpec as P

D = 1024
HEADS = 16
HEAD_DIM = 64
FF = 4096
CLASSES = 1000
FREQ = 256
PATCH = 16
GRID = 16
MICRO = 2
TOKENS_IMG = 256
MAIN = 4 * D + FF
MODS = 6 * D

clip_limit = 0.005
rate = 0.05
decay = 0.01

BOTH = ("dp", "seq")
END_CLASS = CLASSES + 1
END_T1 = END_CLASS + FREQ
END_T2 = END_T1 + D
END_PATCH = END_T2 + PATCH
END_FINAL = END_PATCH + 2 * D


def low(values):
    return values.astype(jnp.bfloat16)


def mm(left, right):
    return jnp.dot(left, right, preferred_element_type=jnp.float32)


def mm_tn(left, right):
    return lax.dot_general(
        left, right, (((0,), (0,)), ((), ())), preferred_element_type=jnp.float32
    )


def mm_nt(left, right):
    return lax.dot_general(
        left, right, (((1,), (1,)), ((), ())), preferred_element_type=jnp.float32
    )


def positions():
    quarter = D // 4
    omegas = 1.0 / 10000.0 ** (jnp.arange(quarter, dtype=jnp.float32) / quarter)
    angles = jnp.arange(GRID, dtype=jnp.int32).astype(jnp.float32)[:, None] * omegas[None, :]
    waves = jnp.concatenate([jnp.sin(angles), jnp.cos(angles)], axis=1)
    whole = (GRID, GRID, 2 * quarter)
    across = jnp.broadcast_to(waves[:, None], whole)
    along = jnp.broadcast_to(waves[None], whole)
    return jnp.concatenate([across, along], axis=2).reshape(TOKENS_IMG, D)


def time_features(time_steps):
    half_freq = FREQ // 2
    rates = jnp.exp(-math.log(10000.0) * jnp.arange(half_freq, dtype=jnp.float32) / half_freq)
    angles = time_steps.astype(jnp.float32)[:, None] * rates[None, :]
    return jnp.concatenate([jnp.cos(angles), jnp.sin(angles)], axis=1)


def signal_levels(time_steps):
    angles = (time_steps.astype(jnp.float32) / 1000.0 + 0.008) / 1.008 * (math.pi / 2.0)
    levels = jnp.cos(angles) ** 2
    return (jnp.sqrt(levels), jnp.sqrt(1.0 - levels))


def norm_stats(values):
    centred = values - jnp.mean(values, axis=-1, keepdims=True)
    inverse = lax.rsqrt(jnp.mean(centred * centred, axis=-1, keepdims=True) + 1e-06)
    return (centred * inverse, inverse)


def norm_back(grad, unit, inverse, scale):
    grad_unit = grad * (1.0 + scale)
    mean_one = jnp.mean(grad_unit, axis=-1, keepdims=True)
    mean_two = jnp.mean(grad_unit * unit, axis=-1, keepdims=True)
    grad_values = inverse * (grad_unit - mean_one - unit * mean_two)
    return (
        grad_values,
        jnp.sum(grad, axis=0, keepdims=True),
        jnp.sum(grad * unit, axis=0, keepdims=True),
    )


GELU_A = math.sqrt(2.0 / math.pi)
GELU_B = 0.044715


def gelu_both(values):
    squared = values * values
    bent = jnp.tanh(GELU_A * (values + GELU_B * squared * values))
    out = 0.5 * values * (1.0 + bent)
    slope = 0.5 * (1.0 + bent) + 0.5 * values * (1.0 - bent * bent) * (
        GELU_A * (1.0 + 3.0 * GELU_B * squared)
    )
    return (out, slope)


def silu_slope(values):
    sig = jax.nn.sigmoid(values)
    return sig * (1.0 + values * (1.0 - sig))


def heads_of(values):
    return values.reshape(values.shape[0], HEADS, HEAD_DIM)


def adam(weight, grad, first_m, second_m, factor, step_count):
    clipped = grad * factor
    first_new = 0.9 * first_m + 0.1 * clipped
    second_new = 0.999 * second_m + 0.001 * clipped * clipped
    first_hat = first_new / (1.0 - 0.9**step_count)
    second_hat = second_new / (1.0 - 0.999**step_count)
    updated = weight - rate * (first_hat / (jnp.sqrt(second_hat) + 1e-08) + decay * weight)
    return (updated, first_new, second_new)


ID_TYPE = pl.DeviceIdType.MESH
LINE = 4


def route():
    me, core = lax.axis_index("dp"), lax.axis_index("seq")
    place, line = me // LINE, me % LINE
    step_x, step_y = 1 - 2 * (line % 2), 2 - 4 * (line // 2)
    near = line + (1 - core) * step_y + core * step_x
    far = line + (1 - core) * step_x + core * step_y
    return core, place, line, near, far, line + step_x + step_y


def transfer(source, target, send_sem, recv_sem, device):
    return pltpu.make_async_remote_copy(
        src_ref=source,
        dst_ref=target,
        send_sem=send_sem,
        recv_sem=recv_sem,
        device_id=device,
        device_id_type=ID_TYPE,
    )


def packed(block):
    groups = [block[..., r : r + 8, :] for r in range(0, 32, 8)]
    return jnp.concatenate(groups, axis=-1)


def unpacked(tiles):
    groups = [tiles[..., c : c + 32] for c in range(0, 128, 32)]
    return jnp.concatenate(groups, axis=-2)


class Exchange:
    def __init__(self, n_dev, send_sem, recv_sem):
        self.n_dev, self.send_sem, self.recv_sem = n_dev, send_sem, recv_sem
        self.me = 2 * lax.axis_index("dp") + lax.axis_index("seq")
        self.started = []

    def greet(self):
        barrier = pltpu.get_barrier_semaphore()
        for k in range(1, self.n_dev):
            other = (self.me + k) % self.n_dev
            pl.semaphore_signal(
                barrier, inc=1, device_id=(other // 2, other % 2), device_id_type=ID_TYPE
            )
        pl.semaphore_wait(barrier, self.n_dev - 1)

    def post(self, row, source, out, each=False):
        sems = (self.send_sem.at[row], self.recv_sem.at[row])
        for k in range(1, self.n_dev):
            other = (self.me + k) % self.n_dev
            block = source.at[other] if each else source
            transfer(block, out.at[self.me], *sems, (other // 2, other % 2)).start()
        out[self.me] = source[self.me] if each else source[...]
        self.started.append((row, out))

    def all_but_one(self, row, out):
        some = out.at[pl.ds(0, self.n_dev - 1)]
        other = (self.me + 1) % self.n_dev
        return transfer(
            some, some, self.send_sem.at[row], self.recv_sem.at[row], (other // 2, other % 2)
        )

    def collect(self, row, out):
        self.all_but_one(row, out).wait_recv()

    def finish(self):
        for row, out in self.started:
            self.all_but_one(row, out).wait_send()


def gather_kernel(pieces, n_dev, *refs):
    wide_in, narrow_in, small, row, class_t, t1_t, t2_t, fs_t, fc_t, bias_t = refs[:10]
    refs = refs[10:]
    wholes, refs = refs[:2], refs[2:]
    small_all, rows_all, time_one, time_all, condition, cond_all, mods_came, final_came, ada = refs[:9]
    main_low, narrow_low, *refs = refs[9:]
    shards = (main_low, narrow_low)
    time_mine, cond_mine, time_came, cond_came, mods_wide, mods_mine, final_mine = refs[:7]
    send_sem, line_sem, near_sem, far_sem, core_sem, own_sem, swap_send, swap_recv = refs[7:]
    swaps = Exchange(n_dev, swap_send, swap_recv)
    total = len(pieces)
    core, place, line, near, far, both = route()
    to_next = (LINE * ((place + 1) % LINE) + line, core)
    to_near, to_far = (LINE * place + near, core), (LINE * place + far, core)
    to_core = (LINE * place + line, 1 - core)

    places = [(place + LINE - j) % LINE for j in range(LINE)]

    def block(piece, j, at, of=None):
        which, cut = pieces[piece]
        return wholes[which].at[(places[j], at, core if of is None else of, *cut)]

    def own_block(piece):
        which, cut = pieces[piece]
        return shards[which].at[cut]

    def own(piece):
        return pltpu.make_async_copy(own_block(piece), block(piece, 0, line), own_sem.at[piece])

    def sent(piece, stage):
        late = piece >= total - AG_LATE and stage < 3
        return send_sem.at[2 if late else pieces[piece][0], stage]

    def hop(piece, j, at, stage, source=None):
        which = pieces[piece][0]
        target = block(piece, j, at)
        if stage == 3:
            arrived = core_sem.at[which]
        elif stage == 2:
            arrived = far_sem.at[piece, j if at is line or at is far else LINE + j]
        else:
            arrived = (line_sem, near_sem)[stage].at[piece, j]
        return transfer(
            target if source is None else source,
            target,
            sent(piece, stage),
            arrived,
            (to_next, to_near, to_far, to_core)[stage],
        )

    def cast(piece):
        which, cut = pieces[piece]
        shards[which][cut] = low((wide_in, narrow_in)[which][cut])

    def start_line(piece):
        cast(piece)
        hop(piece, 0, line, 0, own_block(piece)).start()
        own(piece).start()

    def start_others(piece):
        for stage in (1, 2, 3):
            hop(piece, 0, line, stage, own_block(piece)).start()

    def from_line(j, piece):
        target = block(piece, j, line)
        transfer(target, target, sent(piece, 0), line_sem.at[piece, j - 1], to_next).wait_recv()
        for stage in range(0 if j + 1 < LINE else 1, 4):
            hop(piece, j, line, stage).start()

    def from_near(j, piece):
        hop(piece, j, near, 1).wait_recv()
        hop(piece, j, near, 2).start()
        hop(piece, j, near, 3).start()

    def from_far(j, piece):
        hop(piece, j, far, 2).wait_recv()
        hop(piece, j, far, 3).start()

    def from_both(j, piece):
        hop(piece, j, both, 2).wait_recv()
        hop(piece, j, both, 3).start()

    def ring(piece, j):
        which, cut = pieces[piece]
        four = wholes[which].at[(places[j], slice(None), core, *cut)]
        return transfer(four, four, sent(piece, 0), line_sem.at[piece, j], to_next)

    def start_sides(piece):
        cast(piece)
        own(piece).start()
        start_others(piece)

    def start_ring(piece):
        own(piece).wait()
        ring(piece, 0).start()

    def from_ring(j, piece):
        which, cut = pieces[piece]
        four = wholes[which].at[(places[j], slice(None), core, *cut)]
        transfer(four, four, sent(piece, 0), line_sem.at[piece, j - 1], to_next).wait_recv()
        if j + 1 < LINE:
            ring(piece, j).start()
        transfer(four, four, sent(piece, 3), core_sem.at[which], to_core).start()

    def columns(which):
        return bias_t[:, which : which + 1]

    def time_step():
        for start in range(0, MODS, D):
            ada[:, start : start + D] = low(wide_in[:, MAIN + start : MAIN + start + D])
        swaps.collect(0, rows_all)
        freqs = jnp.concatenate([rows_all[:, 1, :], rows_all[:, 2, :]], axis=1)
        time_one[...] = mm_nt(t1_t[...], low(freqs)) + columns(15)
        time_mine[...] = packed(low(jax.nn.silu(time_one[...])).astype(jnp.float32))
        swaps.post(1, time_mine, time_came)

    def cond_step():
        labels = rows_all[:, 0, :]
        lanes = lax.broadcasted_iota(jnp.int32, labels.shape, 1).astype(jnp.float32)
        chosen = [
            jnp.where(labels == lanes + float(start), 1.0, 0.0)
            for start in range(0, class_t.shape[1], labels.shape[1])
        ]
        swaps.collect(1, time_came)
        time_all[...] = low(unpacked(time_came[...]))
        condition[...] = (
            mm(t2_t[...], time_all[...].reshape(D, n_dev))
            + columns(16)
            + mm_nt(class_t[...], low(jnp.concatenate(chosen, axis=1)))
        )
        act = low(jax.nn.silu(condition[...]))
        cond_mine[...] = packed(act.astype(jnp.float32))
        swaps.post(2, cond_mine, cond_came)
        for start in range(0, MODS, D):
            some = mm_tn(act, ada[:, start : start + D])
            for at in range(0, D, 128):
                mods_wide[:, (start + at) // 128, :] = some[:, at : at + 128]
        mods_mine[...] = low(mods_wide[...])
        swaps.post(3, mods_mine, mods_came, each=True)

    def final_step():
        swaps.collect(2, cond_came)
        cond_all[...] = low(unpacked(cond_came[...]))
        acts = cond_all[...].reshape(D, n_dev)
        both_t = [mm(fs_t[...], acts) + columns(17), mm(fc_t[...], acts) + columns(18)]
        final_mine[:, 0, :] = jnp.concatenate(both_t, axis=0).T
        swaps.post(4, final_mine, final_came, each=True)

    plan = [(AG_EXTRAS[0], time_step), (AG_EXTRAS[1], cond_step), (AG_EXTRAS[2], final_step)]
    for late in range(AG_LATE):
        piece, after = total - AG_LATE + late, late * 12.0 / total
        plan.append((AG_SIDES[0] + after, partial(start_sides, piece)))
        for when, step in zip(AG_SIDES[1:], (from_near, from_far, from_both)):
            plan.append((when + after, partial(step, 0, piece)))
        after *= AG_RING[2]
        plan.append((AG_RING[0] + after, partial(start_ring, piece)))
        for j in range(1, LINE):
            plan.append((AG_RING[0] + AG_RING[1] * j + after, partial(from_ring, j, piece)))
    for piece in range(total - AG_LATE):
        share = piece * 12.0 / total
        plan.append((AG_START[0] * share + AG_START[1], partial(start_line, piece)))
        plan.append((AG_OTHERS[0] * share + AG_OTHERS[1], partial(start_others, piece)))
        for step, (slope, first) in zip((from_line, from_near, from_far, from_both), AG_PLAN):
            for j in range(0 if step is not from_line else 1, LINE):
                plan.append((slope * share + first + AG_HOP * max(j, 1), partial(step, j, piece)))
    swaps.greet()
    swaps.post(0, row.at[core], rows_all)
    swaps.post(5, small, small_all)
    for _, step in sorted(plan, key=lambda planned: planned[0]):
        step()
    for exchange_row, out in ((3, mods_came), (4, final_came), (5, small_all)):
        swaps.collect(exchange_row, out)
    swaps.finish()
    for piece in range(total - AG_LATE):
        own(piece).wait()
    first_late = pieces[total - AG_LATE][1][1].start if AG_LATE else 0
    for which, whole in enumerate(wholes):
        theirs = whole.at[:, :, 1 - core]
        transfer(theirs, theirs, send_sem.at[which, 3], core_sem.at[which], to_core).wait_recv()
        early = (slice(None), slice(0, first_late)) if AG_LATE and which == 0 else (slice(None),) * 2
        spans = (
            whole.at[(pl.ds(0, LINE - 1), 0, 0, *early)],
            whole.at[(slice(None), 0, 0, *early)],
            whole.at[(slice(None), pl.ds(0, 2), 0, *early)],
            whole.at[:, :, 0],
        )
        for stage, span in enumerate(spans):
            transfer(span, span, send_sem.at[which, stage], core_sem.at[which], to_core).wait_send()
    if AG_LATE:
        rest = (slice(None), slice(first_late, MAIN))
        spans = (
            wholes[0].at[(pl.ds(0, LINE - 1), slice(None), 0, *rest)],
            wholes[0].at[(0, 0, 0, *rest)],
            wholes[0].at[(0, pl.ds(0, 2), 0, *rest)],
        )
        for stage, span in enumerate(spans):
            transfer(span, span, send_sem.at[2, stage], core_sem.at[0], to_core).wait_send()


def gather_and_condition(inputs, n_dev, pieces):
    part = D // n_dev
    shards = [(part, MAIN), inputs[1].shape]
    vmem, anywhere = pl.BlockSpec(memory_space=pltpu.VMEM), pl.BlockSpec(memory_space=pl.ANY)
    wide, narrow = jnp.float32, jnp.bfloat16
    out_shape = [jax.ShapeDtypeStruct((LINE, LINE, 2, *s), narrow) for s in shards]
    out_shape += [
        jax.ShapeDtypeStruct((n_dev, *inputs[2].shape), narrow),
        jax.ShapeDtypeStruct((n_dev, *inputs[3].shape[1:]), wide),
        jax.ShapeDtypeStruct((part, n_dev), wide),
        jax.ShapeDtypeStruct((n_dev, part, n_dev), narrow),
        jax.ShapeDtypeStruct((part, n_dev), wide),
        jax.ShapeDtypeStruct((n_dev, part, n_dev), narrow),
        jax.ShapeDtypeStruct((n_dev, MODS // 128, 128), narrow),
        jax.ShapeDtypeStruct((n_dev, 1, 2 * part), wide),
        jax.ShapeDtypeStruct((part, MODS), narrow),
    ]
    return pl.pallas_call(
        partial(gather_kernel, pieces, n_dev),
        out_shape=out_shape,
        in_specs=[vmem] * len(inputs),
        out_specs=[anywhere] * 2 + [vmem] * 9,
        scratch_shapes=[
            *(pltpu.VMEM(s, narrow) for s in shards),
            pltpu.VMEM((8, 128), wide),
            pltpu.VMEM((8, 128), wide),
            pltpu.VMEM((n_dev, 8, 128), wide),
            pltpu.VMEM((n_dev, 8, 128), wide),
            pltpu.VMEM((n_dev, MODS // 128, 128), wide),
            pltpu.VMEM((n_dev, MODS // 128, 128), narrow),
            pltpu.VMEM((n_dev, 1, 2 * part), wide),
            pltpu.SemaphoreType.DMA((3, 4)),
            pltpu.SemaphoreType.DMA((len(pieces), LINE - 1)),
            pltpu.SemaphoreType.DMA((len(pieces), LINE)),
            pltpu.SemaphoreType.DMA((len(pieces), 2 * LINE)),
            pltpu.SemaphoreType.DMA((2,)),
            pltpu.SemaphoreType.DMA((len(pieces),)),
            pltpu.SemaphoreType.DMA((6,)),
            pltpu.SemaphoreType.DMA((6,)),
        ],
        compiler_params=pltpu.CompilerParams(
            collective_id=0, has_side_effects=True, vmem_limit_bytes=58 * 2**20
        ),
    )(*inputs)


def scatter_kernel(pieces, count, n_dev, *refs):
    parts, refs = refs[:count], refs[count:]
    sum_rows, refs = refs[:8], refs[8:]
    inputs, refs = refs[:11], refs[11:]
    mods_low, sums_mine, ada, fs_t, fc_t, t2_t, condition, time_one, cond_all, time_all, rows_all = inputs
    (out_narrow, out_wide, g_class, g_t1, g_t2, g_fs, g_fc), refs = refs[:7], refs[7:]
    small_sum, g_bias, totals = refs[:3]
    mods_all, small_mine, small_all, squares_mine, sums_all, squares_all, small_part = refs[3:10]
    cond_part, cond_came, time_part, time_came, mods_wide, mods_rows, low_cond = refs[10:17]
    refs = refs[17:]
    held, from_core, from_far, from_near, from_line = (
        refs[i * count : (1 + i) * count] for i in range(5)
    )
    send_sem, core_sem, far_sem, near_sem, line_sem, load_sem, swap_send, swap_recv = refs[5 * count :]
    swaps = Exchange(n_dev, swap_send, swap_recv)
    core, place, line, near, far, both = route()
    lanes = (line, near, far, both)
    lanes_there = (line, far, near, both)
    to_near, to_far = (LINE * place + near, core), (LINE * place + far, core)
    to_core = (LINE * place + line, 1 - core)
    order = (3, 2, 1, 0)
    out_at = (0, 4 * D, 3 * D, 0)

    def view(refs_of, piece, *at):
        which, cut = pieces[piece]
        return refs_of[which].at[(*at, *(slice(None) for _ in range(2 - len(at))), *cut)]

    def sent(piece, stage):
        return send_sem.at[pieces[piece][0], stage]

    def over_core(piece, lane):
        which, cut = pieces[piece]
        source = parts[which].at[(slice(None), lanes_there[lane], 1 - core, *cut)]
        target = view(from_core, piece, lane)
        return transfer(source, target, sent(piece, 0), core_sem.at[piece, lane], to_core)

    def load(piece, lane):
        which, cut = pieces[piece]
        source = parts[which].at[(slice(None), lanes[lane], core, *cut)]
        return pltpu.make_async_copy(source, view(held, piece, lane), load_sem.at[piece, lane])

    def over_far(piece):
        which, cut = pieces[piece]
        source = held[which].at[(pl.ds(2, 2), slice(None), *cut)]
        target = from_far[which].at[(pl.ds(0, 2), slice(None), *cut)]
        return transfer(source, target, sent(piece, 1), far_sem.at[piece], to_far)

    def over_near(piece):
        which, cut = pieces[piece]
        source, target = view(held, piece, 1), from_near[which].at[(slice(None), *cut)]
        return transfer(source, target, sent(piece, 2), near_sem.at[piece], to_near)

    def over_line(piece, k):
        which, cut = pieces[piece]
        there = (place + k) % LINE
        source, target = view(held, piece, 0, there), from_line[which].at[(k - 1, *cut)]
        device = (LINE * there + line, core)
        return transfer(source, target, sent(piece, 3), line_sem.at[piece, k - 1], device)

    def add(piece, lane, others_of, *at):
        which, cut = pieces[piece]
        mine, other = held[which], others_of[which]

        def one(i, carry):
            total = mine[(lane, i, *cut)].astype(jnp.float32) + other[(*at, i, *cut)].astype(
                jnp.float32
            )
            mine[(lane, i, *cut)] = total.astype(jnp.bfloat16)
            return carry

        lax.fori_loop(0, LINE, one, 0)

    def begin(piece):
        for lane in order:
            over_core(piece, lane).start()
            load(piece, lane).start()

    def by_core(piece):
        for lane in order:
            load(piece, lane).wait()
            over_core(piece, lane).wait_recv()
            add(piece, lane, from_core, lane)
            if lane == 2:
                over_far(piece).start()

    def by_far(piece):
        over_far(piece).wait_recv()
        add(piece, 1, from_far, 1)
        over_near(piece).start()
        add(piece, 0, from_far, 0)

    def by_near(piece):
        over_near(piece).wait_recv()
        add(piece, 0, from_near)
        for k in range(1, LINE):
            over_line(piece, k).start()

    squares, part = [], D // n_dev

    def squared(values):
        squares.append(jnp.sum(values * values))
        return values

    def by_line(piece):
        which, cut = pieces[piece]
        total = held[which][(0, place, *cut)].astype(jnp.float32)
        for k in range(1, LINE):
            over_line(piece, k).wait_recv()
            total = total + from_line[which][(k - 1, *cut)].astype(jnp.float32)
        squared(total)
        if which == 0:
            out_narrow[cut] = total
        else:
            first = out_at[which] + cut[1].start
            out_wide[:, first : first + total.shape[1]] = total

    def contract_first(left, right, right_dim):
        return lax.dot_general(
            left, right, (((0,), (right_dim,)), ((), ())), preferred_element_type=jnp.float32
        )

    def final_step():
        swaps.collect(2, small_all)
        sums = jnp.sum(small_all[...], axis=0)
        rows = jnp.concatenate([sums[:, c : c + part] for c in (0, 32, 64)], axis=0)
        small_sum[...] = squared(rows)
        by_image = squared(sums[:8, 96:])
        g_bias[:8] = rows[:8]
        g_bias[8:14] = by_image[:6]
        g_bias[14:15] = rows[8:9]
        g_bias[17:19] = by_image[6:]
        shift, scale = low(small_all[:, 6, 96:]), low(small_all[:, 7, 96:])
        back = contract_first(fs_t[...], shift, 1) + contract_first(fc_t[...], scale, 1)
        cond_part[...] = packed(back.reshape(n_dev, part, n_dev))
        swaps.post(4, cond_part, cond_came, each=True)
        acts = cond_all[...].reshape(D, n_dev)
        g_fs[...] = squared(contract_first(shift, acts, 1))
        g_fc[...] = squared(contract_first(scale, acts, 1))

    def cond_step():
        swaps.collect(0, mods_all)
        mods_wide[...] = mods_all[...].astype(jnp.float32)
        for i in range(6):
            mods_rows[:, D * i : D * (i + 1)] = low(mods_wide[:, i, :])
        back = mm_nt(ada[...], mods_rows[...])
        swaps.collect(4, cond_came)
        back = back + unpacked(jnp.sum(cond_came[...], axis=0))
        low_back = low(back * silu_slope(condition[...]))
        low_cond[...] = low_back
        time_part[...] = packed(contract_first(t2_t[...], low_back, 0).reshape(n_dev, part, n_dev))
        swaps.post(5, time_part, time_came, each=True)
        acts = cond_all[swaps.me]
        for start in range(0, MODS, D):
            some = squared(mm(acts, mods_rows[:, start : start + D]))
            out_wide[:, MAIN + start : MAIN + start + D] = some

    def time_step():
        low_back = low_cond[...]
        ones = jnp.ones((8, n_dev), jnp.bfloat16)
        g_bias[16:17] = squared(mm_nt(ones, low_back)[:1])
        labels = rows_all[:, 0, :]
        lanes = lax.broadcasted_iota(jnp.int32, labels.shape, 1).astype(jnp.float32)
        for start in range(0, g_class.shape[1], labels.shape[1]):
            chosen = low(jnp.where(labels == lanes + float(start), 1.0, 0.0))
            g_class[:, start : start + labels.shape[1]] = squared(mm(low_back, chosen))
        g_t2[...] = squared(mm_nt(low_back, time_all[...].reshape(D, n_dev)))
        swaps.collect(3, sums_all)
        swaps.collect(5, time_came)
        low_time = low(unpacked(jnp.sum(time_came[...], axis=0)) * silu_slope(time_one[...]))
        g_bias[15:16] = squared(mm_nt(ones, low_time)[:1])
        freqs = jnp.concatenate([rows_all[:, 1, :], rows_all[:, 2, :]], axis=1)
        g_t1[...] = squared(mm(low_time, low(freqs)))

    total = len(pieces)
    plan = [(RS_EXTRAS[0], final_step), (RS_EXTRAS[1], cond_step), (RS_EXTRAS[2], time_step)]
    for piece in range(total):
        share, when = piece * 12.0 / total, -100.0
        plan.append((RS_BEGIN[0] * share + RS_BEGIN[1], partial(begin, piece)))
        for (slope, first), step in zip(RS_PLAN, (by_core, by_far, by_near, by_line)):
            when = max(when + 0.1, slope * share + first)
            plan.append((when, partial(step, piece)))
    packed_sum, branch_sum, up_sum, down_sum, embed_sum, patch, out_rows, last_rows = sum_rows
    small_part[0:1] = packed_sum[:, :D]
    small_part[1:2] = packed_sum[:, 2 * D :]
    small_part[2:3] = branch_sum[...]
    for i in range(4):
        small_part[3 + i : 4 + i] = up_sum[:, D * i : D * (i + 1)]
    small_part[7:8] = down_sum[...]
    small_part[8:9] = embed_sum[...]
    small_part[9:25] = patch[...]
    small_part[25:41] = out_rows[...]
    small_part[41:48] = last_rows[...]
    small_part[48:56] = mods_low[...].astype(jnp.float32)
    small_part[56:64] = jnp.zeros((8, D), jnp.float32)
    for other in range(n_dev):
        own = slice(other * part, (other + 1) * part)
        groups = [small_part[r : r + 16, own] for r in (0, 16, 32, 48)]
        small_mine[other] = jnp.concatenate(groups, axis=1)
    swaps.greet()
    swaps.post(2, small_mine, small_all, each=True)
    swaps.post(0, mods_low, mods_all)
    swaps.post(3, sums_mine, sums_all)
    for _, step in sorted(plan, key=lambda planned: planned[0]):
        step()
    squares_mine[...] = jnp.broadcast_to(sum(squares), squares_mine.shape)
    swaps.post(6, squares_mine, squares_all)
    sums = jnp.sum(sums_all[...], axis=0)
    lanes = lax.broadcasted_iota(jnp.int32, sums.shape, 1)
    head_sums = jnp.where((lanes >= 1) & (lanes <= PATCH), sums, 0.0)
    swaps.collect(6, squares_all)
    all_squares = jnp.sum(squares_all[...], axis=0) + jnp.sum(head_sums * head_sums)
    totals[0:1] = sums
    totals[1:2] = jnp.sqrt(all_squares)
    swaps.finish()
    for which in range(count):
        for stage, span in enumerate((from_core, from_far, from_near, from_line)):
            transfer(
                span[which], span[which], send_sem.at[which, stage], core_sem.at[0, 0], to_core
            ).wait_send()


def scatter_and_condition(parts, inputs, n_dev, pieces):
    count, part = len(parts), D // n_dev
    shards = [p.shape[3:] for p in parts]
    vmem, anywhere = pl.BlockSpec(memory_space=pltpu.VMEM), pl.BlockSpec(memory_space=pl.ANY)
    wide, narrow = jnp.float32, jnp.bfloat16
    outs = [shards[0], (part, MAIN + MODS)]
    outs += [(part, D), (part, FREQ), (part, D), (part, D), (part, D)]
    outs += [(48, part), (19, part), (2, 128)]
    return pl.pallas_call(
        partial(scatter_kernel, pieces, count, n_dev),
        out_shape=[jax.ShapeDtypeStruct(s, wide) for s in outs],
        in_specs=[anywhere] * count + [vmem] * len(inputs),
        out_specs=[vmem] * len(outs),
        scratch_shapes=[
            pltpu.VMEM((n_dev, 8, D), narrow),
            pltpu.VMEM((n_dev, 16, 128), wide),
            pltpu.VMEM((n_dev, 16, 128), wide),
            pltpu.VMEM((1, 128), wide),
            pltpu.VMEM((n_dev, 1, 128), wide),
            pltpu.VMEM((n_dev, 1, 128), wide),
            pltpu.VMEM((64, D), wide),
            *(pltpu.VMEM((n_dev, 8, 128), wide) for _ in range(4)),
            pltpu.VMEM((n_dev, 8, D), wide),
            pltpu.VMEM((n_dev, MODS), narrow),
            pltpu.VMEM((part, n_dev), narrow),
            *(
                pltpu.VMEM((*blocks, *s), narrow)
                for blocks in ((4, LINE), (4, LINE), (2, LINE), (LINE,), (LINE - 1,))
                for s in shards
            ),
            pltpu.SemaphoreType.DMA((count, 4)),
            pltpu.SemaphoreType.DMA((len(pieces), 4)),
            pltpu.SemaphoreType.DMA((len(pieces),)),
            pltpu.SemaphoreType.DMA((len(pieces),)),
            pltpu.SemaphoreType.DMA((len(pieces), LINE - 1)),
            pltpu.SemaphoreType.DMA((len(pieces), 4)),
            pltpu.SemaphoreType.DMA((7,)),
            pltpu.SemaphoreType.DMA((7,)),
        ],
        compiler_params=pltpu.CompilerParams(
            collective_id=1, has_side_effects=True, vmem_limit_bytes=58 * 2**20
        ),
    )(*parts, *inputs)


AG_START = (4.0, -9.0)
AG_OTHERS = (4.0, -8.5)
AG_HOP = 4.25
AG_PLAN = ((4.0, 0.0), (5.0, 2.0), (5.0, 4.0), (8.5, 8.0))
AG_EXTRAS = (10.0, 25.0, 45.0)
RS_BEGIN = (8.5, -12.0)
RS_PLAN = ((8.5, 0.0), (8.5, 6.5), (8.5, 13.0), (8.5, 19.5))
RS_EXTRAS = (12.0, 30.0, 60.0)
AG_LATE = 4
AG_SIDES = (-9.5, 5.0, 6.0, 12.0)
AG_RING = (20.0, 14.0, 6.0)
AG_CUT = 512
RS_CUT = 512


def tiled(n_dev):
    return n_dev == 8 * LINE and (D // n_dev) % 16 == 0


def column_cuts(which, columns, step):
    return [(which, (slice(None), slice(c, c + step))) for c in range(0, columns, step)]


def row_cuts(which, rows, step):
    return [(which, (slice(r, r + step), slice(None))) for r in range(0, rows, step)]


def first_part(wide, narrow, small, row, table_t, bias_t, n_dev):
    class_t, t1_t, t2_t, fs_t, fc_t = table_t
    if tiled(n_dev):
        pieces = row_cuts(1, FF // n_dev, AG_CUT // 32) + column_cuts(0, MAIN, AG_CUT)
        inputs = [wide, narrow, small.reshape(-1, 128), row, class_t, t1_t, t2_t, fs_t, fc_t, bias_t]
        out = gather_and_condition(inputs, n_dev, tuple(pieces))
        main_all, narrow_all, *rest = out
        return [main_all.reshape(D, MAIN), narrow_all.reshape(FF, D), *rest]
    main_all = lax.all_gather(low(wide[:, :MAIN]), BOTH, axis=0, tiled=True)
    narrow_all = lax.all_gather(low(narrow), BOTH, axis=0, tiled=True)
    ada = low(wide[:, MAIN:])
    small_all = lax.all_gather(small, BOTH)
    rows_all = lax.all_gather(lax.dynamic_index_in_dim(row, lax.axis_index('seq'), 0, False), BOTH)
    freqs = low(rows_all[:, 1:3].reshape(n_dev, FREQ))
    time_one = mm_nt(t1_t, freqs) + bias_t[:, 15:16]
    time_all = lax.all_gather(low(jax.nn.silu(time_one)), BOTH)
    classes = jnp.arange(class_t.shape[1], dtype=jnp.int32).astype(jnp.float32)
    choose = low(rows_all[:, 0, :1] == classes)
    condition = (
        mm(t2_t, time_all.reshape(D, n_dev)) + bias_t[:, 16:17] + mm_nt(class_t, choose)
    )
    cond_mine = low(jax.nn.silu(condition))
    cond_all = lax.all_gather(cond_mine, BOTH)
    mods_mine = low(mm_tn(cond_mine, ada)).reshape(n_dev, MODS // 128, 128)
    mods_came = lax.all_to_all(mods_mine, BOTH, 0, 0, tiled=True)
    acts = cond_all.reshape(D, n_dev)
    both_t = [mm(fs_t, acts) + bias_t[:, 17:18], mm(fc_t, acts) + bias_t[:, 18:19]]
    final_mine = jnp.concatenate(both_t, axis=0).T[:, None]
    final_came = lax.all_to_all(final_mine, BOTH, 0, 0, tiled=True)
    return [main_all, narrow_all, small_all, rows_all, time_one, time_all, condition, cond_all, mods_came, final_came, ada]


def last_part(parts, mods_row, sum_rows, sums_mine, ada, table_t, condition, time_one, cond_all, time_all, rows_all, n_dev):
    _, _, t2_t, fs_t, fc_t = table_t
    mods_low = low(mods_row)
    if tiled(n_dev):
        blocks = [p.reshape(LINE, LINE, 2, p.shape[0] // n_dev, p.shape[1]) for p in parts]
        pieces = row_cuts(0, FF // n_dev, RS_CUT // 32)
        for which in range(1, len(parts)):
            pieces += column_cuts(which, parts[which].shape[1], RS_CUT)
        inputs = [*sum_rows, mods_low, sums_mine, ada, fs_t, fc_t, t2_t, condition, time_one]
        inputs += [cond_all, time_all, rows_all]
        return scatter_and_condition(blocks, inputs, n_dev, tuple(pieces))
    part = D // n_dev
    shards = [
        lax.psum_scatter(p, BOTH, scatter_dimension=0, tiled=True).astype(jnp.float32) for p in parts
    ]

    def by_owner(rows):
        cut = jnp.transpose(rows.reshape(rows.shape[0], n_dev, part), (1, 0, 2))
        return lax.all_to_all(cut, BOTH, 0, 0, tiled=True)

    mods_all = lax.all_gather(mods_low, BOTH).reshape(n_dev, 8 * D)[:, :MODS]
    cut_all = by_owner(mods_low.astype(jnp.float32))
    sum_rows = [sum_rows[0][:, :D], sum_rows[0][:, 2 * D :], *sum_rows[1:]]
    small_part = jnp.concatenate([rows.reshape(-1, D) for rows in sum_rows], axis=0)
    small_sum = jnp.sum(by_owner(small_part), axis=0)
    sums = jnp.sum(lax.all_gather(sums_mine, BOTH), axis=0)
    shift, scale = low(cut_all[:, 6]), low(cut_all[:, 7])
    back = mm(shift, fs_t) + mm(scale, fc_t)
    back = lax.all_to_all(back.T.reshape(n_dev, part, n_dev), BOTH, 0, 0, tiled=True)
    back = jnp.sum(back, axis=0) + mm_nt(ada, mods_all)
    grad_cond = low(back * silu_slope(condition))
    back = mm_tn(t2_t, grad_cond).reshape(n_dev, part, n_dev)
    back = jnp.sum(lax.all_to_all(back, BOTH, 0, 0, tiled=True), axis=0)
    grad_time = low(back * silu_slope(time_one))
    acts = cond_all.reshape(D, n_dev)
    me_cond = lax.dynamic_index_in_dim(cond_all, lax.axis_index(BOTH), 0, keepdims=False)
    classes = jnp.arange(D, dtype=jnp.int32).astype(jnp.float32)
    grads = [
        shards[0],
        jnp.concatenate([shards[3], shards[2], shards[1], mm(me_cond, mods_all)], axis=1),
        mm(grad_cond, low(rows_all[:, 0, :1] == classes)),
        mm(grad_time, low(rows_all[:, 1:3].reshape(n_dev, FREQ))),
        mm_nt(grad_cond, time_all.reshape(D, n_dev)),
        mm(shift.T, acts.T),
        mm(scale.T, acts.T),
        small_sum,
    ]
    cut_sum = jnp.sum(cut_all, axis=0)
    row_of = lambda grad: jnp.sum(grad, axis=1, dtype=jnp.float32)[None]
    bias_rest = [cut_sum, row_of(grad_time), row_of(grad_cond)]
    squares = sum(jnp.sum(g * g) for g in grads + bias_rest)
    squares = jnp.sum(lax.all_gather(squares[None], BOTH)) + jnp.sum(jnp.square(sums[:, 1 : PATCH + 1]))
    g_bias = jnp.concatenate(
        [small_sum[:8], cut_sum[:6], small_sum[8:9], bias_rest[1], bias_rest[2], cut_sum[6:]], axis=0
    )
    return [*grads, g_bias, jnp.concatenate([sums, jnp.full_like(sums, jnp.sqrt(squares))], axis=0)]


def shards(
    latents,
    noises,
    labels,
    dropped,
    timesteps,
    layer_in,
    layer_out,
    cond_table,
    bias_rows,
    head_bias,
    layer_in_m,
    layer_in_v,
    layer_out_m,
    layer_out_v,
    cond_table_m,
    cond_table_v,
    bias_rows_m,
    bias_rows_v,
    head_bias_m,
    head_bias_v,
    adam_step,
):
    core = lax.axis_index("seq")
    chips = lax.axis_size("dp")
    n_dev = chips * lax.axis_size("seq")
    me = lax.axis_index("dp") * 2 + core
    norm_count = float(MICRO * chips * TOKENS_IMG * PATCH)
    part = layer_in.shape[1]

    pair = jnp.concatenate([latents[:, 0], noises[:, 0]], axis=2)
    other = lax.dynamic_index_in_dim(pair, 1 - core, 0, keepdims=False)
    mine = lax.dynamic_index_in_dim(pair, core, 0, keepdims=False)
    came = lax.ppermute(other, "seq", [(0, 1), (1, 0)])
    image = jnp.where(core == 0, jnp.concatenate([mine, came]), jnp.concatenate([came, mine]))
    latent, noise = image[:, :PATCH], image[:, PATCH:]

    classes_own = jnp.where(dropped == 1, CLASSES, labels).astype(jnp.float32)
    freqs_own = low(time_features(timesteps[:, 0])).astype(jnp.float32)
    row = jnp.concatenate(
        [
            jnp.broadcast_to(classes_own[:, :, None], (MICRO, 1, 128)),
            freqs_own.reshape(MICRO, 2, 128),
            jnp.zeros((MICRO, 5, 128)),
        ],
        axis=1,
    )

    table_t = low(cond_table.T)
    bias_low = low(bias_rows)
    bias_t = bias_low.astype(jnp.float32).T

    small = jnp.concatenate(
        [bias_low, table_t[:, END_T2:END_PATCH].T, table_t[:, END_FINAL:].T, jnp.zeros_like(bias_low[:1])],
        axis=0,
    )
    table_parts = (
        jnp.pad(table_t[:, :END_CLASS], ((0, 0), (0, D - END_CLASS))),
        table_t[:, END_CLASS:END_T1],
        table_t[:, END_T1:END_T2],
        table_t[:, END_PATCH : END_PATCH + D],
        table_t[:, END_PATCH + D : END_FINAL],
    )
    (
        main_all,
        narrow_all,
        small_all,
        rows_all,
        time_one,
        time_all,
        condition,
        cond_all,
        mods_came,
        final_came,
        ada_low,
    ) = first_part(layer_in[0], layer_out[0], small, row, table_parts, bias_t, n_dev)
    small_all = jnp.transpose(small_all.reshape(n_dev, 52, part), (1, 0, 2)).reshape(52, D)
    bias_all = small_all[:19].astype(jnp.float32)
    patch_w = small_all[19:35]
    out_w = small_all[35:51]
    mods = (
        jnp.sum(mods_came.astype(jnp.float32), axis=0).reshape(1, MODS)
        + bias_all[8:14].reshape(1, MODS)
    )
    f_shift = final_came[:, 0, :part].reshape(1, D)
    f_scale = final_came[:, 0, part:].reshape(1, D)
    shift_a, scale_a, gate_a, shift_b, scale_b, gate_b = jnp.split(mods, 6, axis=1)

    my_time = jnp.where(core == 0, timesteps[0], timesteps[1])
    keep_level, spread = signal_levels(my_time)
    noisy = low(keep_level[:, None] * latent + spread[:, None] * noise)
    hidden = mm(noisy, patch_w) + bias_all[14] + positions()
    unit_a, inv_a = norm_stats(hidden)
    normed_a = low(unit_a * (1.0 + scale_a) + shift_a)
    bias_qkv = jnp.concatenate([bias_all[0], jnp.zeros((D,), jnp.float32), bias_all[1]])
    packed = low(mm(normed_a, main_all[:, : 3 * D]) + bias_qkv)
    queries, keys, values = (heads_of(packed[:, i * D : (i + 1) * D]) for i in range(3))
    head_scale = 1.0 / math.sqrt(HEAD_DIM)
    scores = (
        jnp.einsum("shd,khd->hsk", queries, keys, preferred_element_type=jnp.float32) * head_scale
    )
    expd = jnp.exp(scores - jnp.max(scores, axis=-1, keepdims=True))
    probs = expd / jnp.sum(expd, axis=-1, keepdims=True)
    probs_low = low(probs)
    attended = jnp.einsum("hsk,khd->shd", probs_low, values, preferred_element_type=jnp.float32)
    attended = low(attended.reshape(TOKENS_IMG, D))
    branch = mm(attended, main_all[:, 3 * D : 4 * D]) + bias_all[2]
    middle = hidden + gate_a * branch
    unit_b, inv_b = norm_stats(middle)
    normed_b = low(unit_b * (1.0 + scale_b) + shift_b)
    upward = mm(normed_b, main_all[:, 4 * D :]) + bias_all[3:7].reshape(FF)
    activated, slope = gelu_both(upward)
    activated = low(activated)
    downward = mm(activated, narrow_all) + bias_all[7]
    last = middle + gate_b * downward
    unit_f, inv_f = norm_stats(last)
    normed_f = low(unit_f * (1.0 + f_scale) + f_shift)
    predicted = mm_nt(normed_f, out_w) + head_bias

    differ = predicted - noise
    loss_part = jnp.sum(differ * differ) / norm_count
    grad_pred = low(2.0 * differ / norm_count)
    head_part = jnp.sum(grad_pred, axis=0, dtype=jnp.float32)
    grad_out_w = mm_tn(grad_pred, normed_f)
    grad_last, g_fshift, g_fscale = norm_back(mm(grad_pred, out_w), unit_f, inv_f, f_scale)
    g_gate_b = jnp.sum(grad_last * downward, axis=0, keepdims=True)
    grad_down = low(gate_b * grad_last)
    grad_narrow = low(mm_tn(activated, grad_down))
    grad_up = low(slope * mm_nt(grad_down, narrow_all))
    grad_fc1 = low(mm_tn(normed_b, grad_up))
    grad_mid, g_shift_b, g_scale_b = norm_back(
        mm_nt(grad_up, main_all[:, 4 * D :]), unit_b, inv_b, scale_b
    )
    grad_middle = grad_last + grad_mid
    g_gate_a = jnp.sum(grad_middle * branch, axis=0, keepdims=True)
    grad_branch = low(gate_a * grad_middle)
    grad_proj = low(mm_tn(attended, grad_branch))
    grad_att = heads_of(low(mm_nt(grad_branch, main_all[:, 3 * D : 4 * D])))
    grad_probs = jnp.einsum("shd,khd->hsk", grad_att, values, preferred_element_type=jnp.float32)
    grad_values = jnp.einsum("hsk,shd->khd", probs_low, grad_att, preferred_element_type=jnp.float32)
    grad_scores = low(
        probs * (grad_probs - jnp.sum(grad_probs * probs, axis=-1, keepdims=True))
    )
    grad_queries = (
        jnp.einsum("hsk,khd->shd", grad_scores, keys, preferred_element_type=jnp.float32)
        * head_scale
    )
    grad_keys = (
        jnp.einsum("hsk,shd->khd", grad_scores, queries, preferred_element_type=jnp.float32)
        * head_scale
    )
    grad_packed = low(
        jnp.concatenate(
            [g.reshape(TOKENS_IMG, D) for g in (grad_queries, grad_keys, grad_values)], axis=1
        )
    )
    grad_qkv = low(mm_tn(normed_a, grad_packed))
    grad_hid, g_shift_a, g_scale_a = norm_back(
        mm_nt(grad_packed, main_all[:, : 3 * D]), unit_a, inv_a, scale_a
    )
    grad_embed = low(grad_middle + grad_hid)
    grad_patch = mm_tn(noisy, grad_embed)

    row_sums = lambda values: jnp.sum(values.astype(jnp.float32), axis=0, keepdims=True)
    sum_rows = [
        row_sums(grad_packed),
        row_sums(grad_branch),
        row_sums(grad_up),
        row_sums(grad_down),
        row_sums(grad_embed),
        grad_patch,
        grad_out_w,
        jnp.zeros((7, D)),
    ]
    sums_mine = jnp.pad(jnp.concatenate([loss_part[None], head_part]), (0, 111))[None]
    mods_row = low(
        jnp.concatenate(
            [g_shift_a, g_scale_a, g_gate_a, g_shift_b, g_scale_b, g_gate_b, g_fshift, g_fscale],
            axis=0,
        )
    )
    (
        grad_narrow,
        grad_wide,
        grad_class,
        grad_t1,
        grad_t2,
        grad_fs,
        grad_fc,
        small_sum,
        grad_bias,
        totals,
    ) = last_part(
        [grad_narrow, grad_fc1, grad_proj, grad_qkv],
        mods_row,
        sum_rows,
        sums_mine,
        ada_low,
        table_parts,
        condition,
        time_one,
        cond_all,
        time_all,
        rows_all,
        n_dev,
    )
    loss_total, head_total = totals[0, 0], totals[0, 1 : PATCH + 1]
    grad_table = jnp.concatenate(
        [
            grad_class[:, :END_CLASS],
            grad_t1,
            grad_t2,
            small_sum[9:25].T,
            grad_fs,
            grad_fc,
            small_sum[25:41].T,
        ],
        axis=1,
    ).T
    grad_wide, grad_narrow = grad_wide[None], grad_narrow[None]
    norm = totals[1, 0]
    factor = jnp.minimum(1.0, clip_limit / (norm + 1e-06))
    step_count = adam_step[0].astype(jnp.float32)
    results = [loss_total, norm]
    results.extend(adam(layer_in, grad_wide, layer_in_m, layer_in_v, factor, step_count))
    results.extend(adam(layer_out, grad_narrow, layer_out_m, layer_out_v, factor, step_count))
    results.extend(adam(cond_table, grad_table, cond_table_m, cond_table_v, factor, step_count))
    results.extend(adam(bias_rows, grad_bias, bias_rows_m, bias_rows_v, factor, step_count))
    results.extend(adam(head_bias, head_total, head_bias_m, head_bias_v, factor, step_count))
    return tuple(results)


def solution(mesh):
    in_specs = (
        P(None, "dp", "seq", None),
        P(None, "dp", "seq", None),
        P(None, "dp"),
        P(None, "dp"),
        P(None, "dp"),
        P(None, ("dp", "seq"), None),
        P(None, ("dp", "seq"), None),
        P(None, ("dp", "seq")),
        P(None, ("dp", "seq")),
        P(),
        P(None, ("dp", "seq"), None),
        P(None, ("dp", "seq"), None),
        P(None, ("dp", "seq"), None),
        P(None, ("dp", "seq"), None),
        P(None, ("dp", "seq")),
        P(None, ("dp", "seq")),
        P(None, ("dp", "seq")),
        P(None, ("dp", "seq")),
        P(),
        P(),
        P(),
    )
    out_specs = (
        P(),
        P(),
        P(None, ("dp", "seq"), None),
        P(None, ("dp", "seq"), None),
        P(None, ("dp", "seq"), None),
        P(None, ("dp", "seq"), None),
        P(None, ("dp", "seq"), None),
        P(None, ("dp", "seq"), None),
        P(None, ("dp", "seq")),
        P(None, ("dp", "seq")),
        P(None, ("dp", "seq")),
        P(None, ("dp", "seq")),
        P(None, ("dp", "seq")),
        P(None, ("dp", "seq")),
        P(),
        P(),
        P(),
    )
    return jax.shard_map(shards, mesh=mesh, in_specs=in_specs, out_specs=out_specs, check_vma=False)
```

```python
from functools import partial
import math

import jax
import jax.numpy as jnp
from jax import lax
from jax.experimental import pallas as pl
from jax.experimental.pallas import tpu as pltpu
from jax.sharding import PartitionSpec as P

D = 1024
HEADS = 16
HEAD_DIM = 64
FF = 4096
CLASSES = 1000
FREQ = 256
PATCH = 16
GRID = 16
MICRO = 2
TOKENS_IMG = 256
MAIN = 4 * D + FF
MODS = 6 * D

clip_limit = 0.005
rate = 0.05
decay = 0.01

BOTH = ("dp", "seq")
END_CLASS = CLASSES + 1
END_T1 = END_CLASS + FREQ
END_T2 = END_T1 + D
END_PATCH = END_T2 + PATCH
END_FINAL = END_PATCH + 2 * D


def low(values):
    return values.astype(jnp.bfloat16)


def mm(left, right):
    return jnp.dot(left, right, preferred_element_type=jnp.float32)


def mm_tn(left, right):
    return lax.dot_general(
        left, right, (((0,), (0,)), ((), ())), preferred_element_type=jnp.float32
    )


def mm_nt(left, right):
    return lax.dot_general(
        left, right, (((1,), (1,)), ((), ())), preferred_element_type=jnp.float32
    )


def positions():
    quarter = D // 4
    omegas = 1.0 / 10000.0 ** (jnp.arange(quarter, dtype=jnp.float32) / quarter)
    angles = jnp.arange(GRID, dtype=jnp.int32).astype(jnp.float32)[:, None] * omegas[None, :]
    waves = jnp.concatenate([jnp.sin(angles), jnp.cos(angles)], axis=1)
    whole = (GRID, GRID, 2 * quarter)
    across = jnp.broadcast_to(waves[:, None], whole)
    along = jnp.broadcast_to(waves[None], whole)
    return jnp.concatenate([across, along], axis=2).reshape(TOKENS_IMG, D)


def time_features(time_steps):
    half_freq = FREQ // 2
    rates = jnp.exp(-math.log(10000.0) * jnp.arange(half_freq, dtype=jnp.float32) / half_freq)
    angles = time_steps.astype(jnp.float32)[:, None] * rates[None, :]
    return jnp.concatenate([jnp.cos(angles), jnp.sin(angles)], axis=1)


def signal_levels(time_steps):
    angles = (time_steps.astype(jnp.float32) / 1000.0 + 0.008) / 1.008 * (math.pi / 2.0)
    levels = jnp.cos(angles) ** 2
    return (jnp.sqrt(levels), jnp.sqrt(1.0 - levels))


def norm_stats(values):
    centred = values - jnp.mean(values, axis=-1, keepdims=True)
    inverse = lax.rsqrt(jnp.mean(centred * centred, axis=-1, keepdims=True) + 1e-06)
    return (centred * inverse, inverse)


def norm_back(grad, unit, inverse, scale):
    grad_unit = grad * (1.0 + scale)
    mean_one = jnp.mean(grad_unit, axis=-1, keepdims=True)
    mean_two = jnp.mean(grad_unit * unit, axis=-1, keepdims=True)
    grad_values = inverse * (grad_unit - mean_one - unit * mean_two)
    return (
        grad_values,
        jnp.sum(grad, axis=0, keepdims=True),
        jnp.sum(grad * unit, axis=0, keepdims=True),
    )


GELU_A = math.sqrt(2.0 / math.pi)
GELU_B = 0.044715


def gelu_both(values):
    squared = values * values
    bent = jnp.tanh(GELU_A * (values + GELU_B * squared * values))
    out = 0.5 * values * (1.0 + bent)
    slope = 0.5 * (1.0 + bent) + 0.5 * values * (1.0 - bent * bent) * (
        GELU_A * (1.0 + 3.0 * GELU_B * squared)
    )
    return (out, slope)


def silu_slope(values):
    sig = jax.nn.sigmoid(values)
    return sig * (1.0 + values * (1.0 - sig))


def heads_of(values):
    return values.reshape(values.shape[0], HEADS, HEAD_DIM)


def adam(weight, grad, first_m, second_m, factor, step_count):
    clipped = grad * factor
    first_new = 0.9 * first_m + 0.1 * clipped
    second_new = 0.999 * second_m + 0.001 * clipped * clipped
    first_hat = first_new / (1.0 - 0.9**step_count)
    second_hat = second_new / (1.0 - 0.999**step_count)
    updated = weight - rate * (first_hat / (jnp.sqrt(second_hat) + 1e-08) + decay * weight)
    return (updated, first_new, second_new)


ID_TYPE = pl.DeviceIdType.MESH
LINE = 4


def route():
    me, core = lax.axis_index("dp"), lax.axis_index("seq")
    place, line = me // LINE, me % LINE
    step_x, step_y = 1 - 2 * (line % 2), 2 - 4 * (line // 2)
    near = line + (1 - core) * step_y + core * step_x
    far = line + (1 - core) * step_x + core * step_y
    return core, place, line, near, far, line + step_x + step_y


def transfer(source, target, send_sem, recv_sem, device):
    return pltpu.make_async_remote_copy(
        src_ref=source,
        dst_ref=target,
        send_sem=send_sem,
        recv_sem=recv_sem,
        device_id=device,
        device_id_type=ID_TYPE,
    )


def packed(block):
    groups = [block[..., r : r + 8, :] for r in range(0, 32, 8)]
    return jnp.concatenate(groups, axis=-1)


def unpacked(tiles):
    groups = [tiles[..., c : c + 32] for c in range(0, 128, 32)]
    return jnp.concatenate(groups, axis=-2)


class Exchange:
    def __init__(self, n_dev, send_sem, recv_sem):
        self.n_dev, self.send_sem, self.recv_sem = n_dev, send_sem, recv_sem
        self.me = 2 * lax.axis_index("dp") + lax.axis_index("seq")
        self.started = []

    def greet(self):
        barrier = pltpu.get_barrier_semaphore()
        for k in range(1, self.n_dev):
            other = (self.me + k) % self.n_dev
            pl.semaphore_signal(
                barrier, inc=1, device_id=(other // 2, other % 2), device_id_type=ID_TYPE
            )
        pl.semaphore_wait(barrier, self.n_dev - 1)

    def post(self, row, source, out, each=False):
        sems = (self.send_sem.at[row], self.recv_sem.at[row])
        for k in range(1, self.n_dev):
            other = (self.me + k) % self.n_dev
            block = source.at[other] if each else source
            transfer(block, out.at[self.me], *sems, (other // 2, other % 2)).start()
        out[self.me] = source[self.me] if each else source[...]
        self.started.append((row, out))

    def all_but_one(self, row, out):
        some = out.at[pl.ds(0, self.n_dev - 1)]
        other = (self.me + 1) % self.n_dev
        return transfer(
            some, some, self.send_sem.at[row], self.recv_sem.at[row], (other // 2, other % 2)
        )

    def collect(self, row, out):
        self.all_but_one(row, out).wait_recv()

    def finish(self):
        for row, out in self.started:
            self.all_but_one(row, out).wait_send()


def gather_kernel(pieces, n_dev, *refs):
    wide_in, narrow_in, small, row, class_t, t1_t, t2_t, fs_t, fc_t, bias_t = refs[:10]
    refs = refs[10:]
    wholes, refs = refs[:2], refs[2:]
    small_rows, rows_all, time_one, time_all, condition, cond_all, mods_sum, final_came, ada, levels = (
        refs[:10]
    )
    main_low, narrow_low, small_all, mods_came, *refs = refs[10:]
    shards = (main_low, narrow_low)
    time_mine, cond_mine, time_came, cond_came, mods_wide, mods_mine, final_mine = refs[:7]
    send_sem, line_sem, near_sem, far_sem, core_sem, own_sem, swap_send, swap_recv = refs[7:]
    swaps = Exchange(n_dev, swap_send, swap_recv)
    total = len(pieces)
    core, place, line, near, far, both = route()
    to_next = (LINE * ((place + 1) % LINE) + line, core)
    to_near, to_far = (LINE * place + near, core), (LINE * place + far, core)
    to_core = (LINE * place + line, 1 - core)

    places = [(place + LINE - j) % LINE for j in range(LINE)]

    def block(piece, j, at, of=None):
        which, cut = pieces[piece]
        return wholes[which].at[(places[j], at, core if of is None else of, *cut)]

    def own_block(piece):
        which, cut = pieces[piece]
        return shards[which].at[cut]

    def own(piece):
        return pltpu.make_async_copy(own_block(piece), block(piece, 0, line), own_sem.at[piece])

    def sent(piece, stage):
        late = piece >= total - AG_LATE and stage < 3
        return send_sem.at[2 if late else pieces[piece][0], stage]

    def hop(piece, j, at, stage, source=None):
        which = pieces[piece][0]
        target = block(piece, j, at)
        if stage == 3:
            arrived = core_sem.at[which]
        elif stage == 2:
            arrived = far_sem.at[piece, j if at is line or at is far else LINE + j]
        else:
            arrived = (line_sem, near_sem)[stage].at[piece, j]
        return transfer(
            target if source is None else source,
            target,
            sent(piece, stage),
            arrived,
            (to_next, to_near, to_far, to_core)[stage],
        )

    def cast(piece):
        which, cut = pieces[piece]
        shards[which][cut] = low((wide_in, narrow_in)[which][cut])

    def start_line(piece):
        cast(piece)
        hop(piece, 0, line, 0, own_block(piece)).start()
        own(piece).start()

    def start_others(piece):
        for stage in (1, 2, 3):
            hop(piece, 0, line, stage, own_block(piece)).start()

    def from_line(j, piece):
        target = block(piece, j, line)
        transfer(target, target, sent(piece, 0), line_sem.at[piece, j - 1], to_next).wait_recv()
        for stage in range(0 if j + 1 < LINE else 1, 4):
            hop(piece, j, line, stage).start()

    def from_near(j, piece):
        hop(piece, j, near, 1).wait_recv()
        hop(piece, j, near, 2).start()
        hop(piece, j, near, 3).start()

    def from_far(j, piece):
        hop(piece, j, far, 2).wait_recv()
        hop(piece, j, far, 3).start()

    def from_both(j, piece):
        hop(piece, j, both, 2).wait_recv()
        hop(piece, j, both, 3).start()

    def ring(piece, j):
        which, cut = pieces[piece]
        four = wholes[which].at[(places[j], slice(None), core, *cut)]
        return transfer(four, four, sent(piece, 0), line_sem.at[piece, j], to_next)

    def start_sides(piece):
        cast(piece)
        own(piece).start()
        start_others(piece)

    def start_ring(piece):
        own(piece).wait()
        ring(piece, 0).start()

    def from_ring(j, piece):
        which, cut = pieces[piece]
        four = wholes[which].at[(places[j], slice(None), core, *cut)]
        transfer(four, four, sent(piece, 0), line_sem.at[piece, j - 1], to_next).wait_recv()
        if j + 1 < LINE:
            ring(piece, j).start()
        transfer(four, four, sent(piece, 3), core_sem.at[which], to_core).start()

    def columns(which):
        return bias_t[:, which : which + 1]

    def time_step():
        for start in range(0, MODS, D):
            ada[:, start : start + D] = low(wide_in[:, MAIN + start : MAIN + start + D])
        swaps.collect(0, rows_all)
        freqs = jnp.concatenate([rows_all[:, 1, :], rows_all[:, 2, :]], axis=1)
        time_one[...] = mm_nt(t1_t[...], low(freqs)) + columns(15)
        time_mine[...] = packed(low(jax.nn.silu(time_one[...])).astype(jnp.float32))
        swaps.post(1, time_mine, time_came)

    def cond_step():
        labels = rows_all[:, 0, :]
        lanes = lax.broadcasted_iota(jnp.int32, labels.shape, 1).astype(jnp.float32)
        chosen = [
            jnp.where(labels == lanes + float(start), 1.0, 0.0)
            for start in range(0, class_t.shape[1], labels.shape[1])
        ]
        swaps.collect(1, time_came)
        time_all[...] = low(unpacked(time_came[...]))
        condition[...] = (
            mm(t2_t[...], time_all[...].reshape(D, n_dev))
            + columns(16)
            + mm_nt(class_t[...], low(jnp.concatenate(chosen, axis=1)))
        )
        act = low(jax.nn.silu(condition[...]))
        cond_mine[...] = packed(act.astype(jnp.float32))
        swaps.post(2, cond_mine, cond_came)
        for start in range(0, MODS, D):
            some = mm_tn(act, ada[:, start : start + D])
            for at in range(0, D, 128):
                mods_wide[:, (start + at) // 128, :] = some[:, at : at + 128]
        mods_mine[...] = low(mods_wide[...])
        swaps.post(3, mods_mine, mods_came, each=True)

    def final_step():
        swaps.collect(2, cond_came)
        cond_all[...] = low(unpacked(cond_came[...]))
        acts = cond_all[...].reshape(D, n_dev)
        both_t = [mm(fs_t[...], acts) + columns(17), mm(fc_t[...], acts) + columns(18)]
        final_mine[:, 0, :] = jnp.concatenate(both_t, axis=0).T
        swaps.post(4, final_mine, final_came, each=True)

    def sums_step():
        swaps.collect(3, mods_came)
        sums = mods_came[0].astype(jnp.float32)
        for other in range(1, n_dev):
            sums = sums + mods_came[other].astype(jnp.float32)
        mods_sum[...] = sums
        swaps.collect(5, small_all)
        for group in range(4):
            own_lanes = slice(32 * group, 32 * group + 32)
            for first in range(0, n_dev, 4):
                tile = [small_all[first + i][:, own_lanes] for i in range(4)]
                small_rows[16 * group : 16 * group + 16, 32 * first : 32 * first + 128] = (
                    jnp.concatenate(tile, axis=1)
                )

    plan = [(AG_EXTRAS[0], time_step), (AG_EXTRAS[1], cond_step), (AG_EXTRAS[2], final_step)]
    plan.append((AG_EXTRAS[3], sums_step))
    for late in range(AG_LATE):
        piece, after = total - AG_LATE + late, late * 12.0 / total
        plan.append((AG_SIDES[0] + after, partial(start_sides, piece)))
        for when, step in zip(AG_SIDES[1:], (from_near, from_far, from_both)):
            plan.append((when + after, partial(step, 0, piece)))
        after *= AG_RING[2]
        plan.append((AG_RING[0] + after, partial(start_ring, piece)))
        for j in range(1, LINE):
            plan.append((AG_RING[0] + AG_RING[1] * j + after, partial(from_ring, j, piece)))
    for piece in range(total - AG_LATE):
        share = piece * 12.0 / total
        plan.append((AG_START[0] * share + AG_START[1], partial(start_line, piece)))
        plan.append((AG_OTHERS[0] * share + AG_OTHERS[1], partial(start_others, piece)))
        for step, (slope, first) in zip((from_line, from_near, from_far, from_both), AG_PLAN):
            for j in range(0 if step is not from_line else 1, LINE):
                plan.append((slope * share + first + AG_HOP * max(j, 1), partial(step, j, piece)))
    swaps.greet()
    swaps.post(0, row.at[core], rows_all)
    levels[...] = row[core]
    swaps.post(5, small, small_all)
    for _, step in sorted(plan, key=lambda planned: planned[0]):
        step()
    swaps.collect(4, final_came)
    swaps.finish()
    for piece in range(total - AG_LATE):
        own(piece).wait()
    first_late = pieces[total - AG_LATE][1][1].start if AG_LATE else 0
    for which, whole in enumerate(wholes):
        theirs = whole.at[:, :, 1 - core]
        transfer(theirs, theirs, send_sem.at[which, 3], core_sem.at[which], to_core).wait_recv()
        early = (slice(None), slice(0, first_late)) if AG_LATE and which == 0 else (slice(None),) * 2
        spans = (
            whole.at[(pl.ds(0, LINE - 1), 0, 0, *early)],
            whole.at[(slice(None), 0, 0, *early)],
            whole.at[(slice(None), pl.ds(0, 2), 0, *early)],
            whole.at[:, :, 0],
        )
        for stage, span in enumerate(spans):
            transfer(span, span, send_sem.at[which, stage], core_sem.at[which], to_core).wait_send()
    if AG_LATE:
        rest = (slice(None), slice(first_late, MAIN))
        spans = (
            wholes[0].at[(pl.ds(0, LINE - 1), slice(None), 0, *rest)],
            wholes[0].at[(0, 0, 0, *rest)],
            wholes[0].at[(0, pl.ds(0, 2), 0, *rest)],
        )
        for stage, span in enumerate(spans):
            transfer(span, span, send_sem.at[2, stage], core_sem.at[0], to_core).wait_send()


def gather_and_condition(inputs, n_dev, pieces):
    part = D // n_dev
    shards = [(part, MAIN), inputs[1].shape]
    vmem, anywhere = pl.BlockSpec(memory_space=pltpu.VMEM), pl.BlockSpec(memory_space=pl.ANY)
    wide, narrow = jnp.float32, jnp.bfloat16
    out_shape = [jax.ShapeDtypeStruct((LINE, LINE, 2, *s), narrow) for s in shards]
    out_shape += [
        jax.ShapeDtypeStruct((4 * inputs[2].shape[0], D), narrow),
        jax.ShapeDtypeStruct((n_dev, *inputs[3].shape[1:]), wide),
        jax.ShapeDtypeStruct((part, n_dev), wide),
        jax.ShapeDtypeStruct((n_dev, part, n_dev), narrow),
        jax.ShapeDtypeStruct((part, n_dev), wide),
        jax.ShapeDtypeStruct((n_dev, part, n_dev), narrow),
        jax.ShapeDtypeStruct((MODS // 128, 128), wide),
        jax.ShapeDtypeStruct((n_dev, 1, 2 * part), wide),
        jax.ShapeDtypeStruct((part, MODS), narrow),
        jax.ShapeDtypeStruct(inputs[3].shape[1:], wide),
    ]
    return pl.pallas_call(
        partial(gather_kernel, pieces, n_dev),
        out_shape=out_shape,
        in_specs=[vmem] * len(inputs),
        out_specs=[anywhere] * 2 + [vmem] * 10,
        scratch_shapes=[
            *(pltpu.VMEM(s, narrow) for s in shards),
            pltpu.VMEM((n_dev, *inputs[2].shape), narrow),
            pltpu.VMEM((n_dev, MODS // 128, 128), narrow),
            pltpu.VMEM((8, 128), wide),
            pltpu.VMEM((8, 128), wide),
            pltpu.VMEM((n_dev, 8, 128), wide),
            pltpu.VMEM((n_dev, 8, 128), wide),
            pltpu.VMEM((n_dev, MODS // 128, 128), wide),
            pltpu.VMEM((n_dev, MODS // 128, 128), narrow),
            pltpu.VMEM((n_dev, 1, 2 * part), wide),
            pltpu.SemaphoreType.DMA((3, 4)),
            pltpu.SemaphoreType.DMA((len(pieces), LINE - 1)),
            pltpu.SemaphoreType.DMA((len(pieces), LINE)),
            pltpu.SemaphoreType.DMA((len(pieces), 2 * LINE)),
            pltpu.SemaphoreType.DMA((2,)),
            pltpu.SemaphoreType.DMA((len(pieces),)),
            pltpu.SemaphoreType.DMA((6,)),
            pltpu.SemaphoreType.DMA((6,)),
        ],
        compiler_params=pltpu.CompilerParams(
            collective_id=0, has_side_effects=True, vmem_limit_bytes=58 * 2**20
        ),
    )(*inputs)


def scatter_kernel(pieces, count, n_dev, *refs):
    parts, refs = refs[:count], refs[count:]
    sum_rows, refs = refs[:8], refs[8:]
    inputs, refs = refs[:11], refs[11:]
    mods_low, sums_mine, ada, fs_t, fc_t, t2_t, condition, time_one, cond_all, time_all, rows_all = inputs
    (out_narrow, out_wide, g_class, g_t1, g_t2, g_fs, g_fc), refs = refs[:7], refs[7:]
    small_sum, g_bias, totals = refs[:3]
    mods_all, small_mine, small_all, squares_mine, sums_all, squares_all, small_part = refs[3:10]
    cond_part, cond_came, time_part, time_came, mods_wide, mods_rows, low_cond = refs[10:17]
    refs = refs[17:]
    held, from_core, from_far, from_near, from_line = (
        refs[i * count : (1 + i) * count] for i in range(5)
    )
    send_sem, core_sem, far_sem, near_sem, line_sem, load_sem, swap_send, swap_recv = refs[5 * count :]
    swaps = Exchange(n_dev, swap_send, swap_recv)
    core, place, line, near, far, both = route()
    lanes = (line, near, far, both)
    lanes_there = (line, far, near, both)
    to_near, to_far = (LINE * place + near, core), (LINE * place + far, core)
    to_core = (LINE * place + line, 1 - core)
    order = (3, 2, 1, 0)
    out_at = (0, 4 * D, 3 * D, 0)

    def view(refs_of, piece, *at):
        which, cut = pieces[piece]
        return refs_of[which].at[(*at, *(slice(None) for _ in range(2 - len(at))), *cut)]

    def sent(piece, stage):
        return send_sem.at[pieces[piece][0], stage]

    def over_core(piece, lane):
        which, cut = pieces[piece]
        source = parts[which].at[(slice(None), lanes_there[lane], 1 - core, *cut)]
        target = view(from_core, piece, lane)
        return transfer(source, target, sent(piece, 0), core_sem.at[piece, lane], to_core)

    def load(piece, lane):
        which, cut = pieces[piece]
        source = parts[which].at[(slice(None), lanes[lane], core, *cut)]
        return pltpu.make_async_copy(source, view(held, piece, lane), load_sem.at[piece, lane])

    def over_far(piece):
        which, cut = pieces[piece]
        source = held[which].at[(pl.ds(2, 2), slice(None), *cut)]
        target = from_far[which].at[(pl.ds(0, 2), slice(None), *cut)]
        return transfer(source, target, sent(piece, 1), far_sem.at[piece], to_far)

    def over_near(piece):
        which, cut = pieces[piece]
        source, target = view(held, piece, 1), from_near[which].at[(slice(None), *cut)]
        return transfer(source, target, sent(piece, 2), near_sem.at[piece], to_near)

    def over_line(piece, k):
        which, cut = pieces[piece]
        there = (place + k) % LINE
        source, target = view(held, piece, 0, there), from_line[which].at[(k - 1, *cut)]
        device = (LINE * there + line, core)
        return transfer(source, target, sent(piece, 3), line_sem.at[piece, k - 1], device)

    def add(piece, lane, others_of, *at):
        which, cut = pieces[piece]
        mine, other = held[which], others_of[which]

        def one(i, carry):
            total = mine[(lane, i, *cut)].astype(jnp.float32) + other[(*at, i, *cut)].astype(
                jnp.float32
            )
            mine[(lane, i, *cut)] = total.astype(jnp.bfloat16)
            return carry

        lax.fori_loop(0, LINE, one, 0)

    def begin(piece):
        for lane in order:
            over_core(piece, lane).start()
            load(piece, lane).start()

    def by_core(piece):
        for lane in order:
            load(piece, lane).wait()
            over_core(piece, lane).wait_recv()
            add(piece, lane, from_core, lane)
            if lane == 2:
                over_far(piece).start()

    def by_far(piece):
        over_far(piece).wait_recv()
        add(piece, 1, from_far, 1)
        over_near(piece).start()
        add(piece, 0, from_far, 0)

    def by_near(piece):
        over_near(piece).wait_recv()
        add(piece, 0, from_near)
        for k in range(1, LINE):
            over_line(piece, k).start()

    squares, part = [], D // n_dev

    def squared(values):
        squares.append(jnp.sum(values * values))
        return values

    def by_line(piece):
        which, cut = pieces[piece]
        total = held[which][(0, place, *cut)].astype(jnp.float32)
        for k in range(1, LINE):
            over_line(piece, k).wait_recv()
            total = total + from_line[which][(k - 1, *cut)].astype(jnp.float32)
        squared(total)
        if which == 0:
            out_narrow[cut] = total
        else:
            first = out_at[which] + cut[1].start
            out_wide[:, first : first + total.shape[1]] = total

    def contract_first(left, right, right_dim):
        return lax.dot_general(
            left, right, (((0,), (right_dim,)), ((), ())), preferred_element_type=jnp.float32
        )

    def final_step():
        swaps.collect(2, small_all)
        sums = jnp.sum(small_all[...], axis=0)
        rows = jnp.concatenate([sums[:, c : c + part] for c in (0, 32, 64)], axis=0)
        small_sum[...] = squared(rows)
        by_image = squared(sums[:8, 96:])
        g_bias[:8] = rows[:8]
        g_bias[8:14] = by_image[:6]
        g_bias[14:15] = rows[8:9]
        g_bias[17:19] = by_image[6:]
        shift, scale = low(small_all[:, 6, 96:]), low(small_all[:, 7, 96:])
        back = contract_first(fs_t[...], shift, 1) + contract_first(fc_t[...], scale, 1)
        cond_part[...] = packed(back.reshape(n_dev, part, n_dev))
        swaps.post(4, cond_part, cond_came, each=True)
        acts = cond_all[...].reshape(D, n_dev)
        g_fs[...] = squared(contract_first(shift, acts, 1))
        g_fc[...] = squared(contract_first(scale, acts, 1))

    def cond_step():
        swaps.collect(0, mods_all)
        mods_wide[...] = mods_all[...].astype(jnp.float32)
        for i in range(6):
            mods_rows[:, D * i : D * (i + 1)] = low(mods_wide[:, i, :])
        back = mm_nt(ada[...], mods_rows[...])
        swaps.collect(4, cond_came)
        back = back + unpacked(jnp.sum(cond_came[...], axis=0))
        low_back = low(back * silu_slope(condition[...]))
        low_cond[...] = low_back
        time_part[...] = packed(contract_first(t2_t[...], low_back, 0).reshape(n_dev, part, n_dev))
        swaps.post(5, time_part, time_came, each=True)
        acts = cond_all[swaps.me]
        for start in range(0, MODS, D):
            some = squared(mm(acts, mods_rows[:, start : start + D]))
            out_wide[:, MAIN + start : MAIN + start + D] = some

    def time_step():
        low_back = low_cond[...]
        ones = jnp.ones((8, n_dev), jnp.bfloat16)
        g_bias[16:17] = squared(mm_nt(ones, low_back)[:1])
        labels = rows_all[:, 0, :]
        lanes = lax.broadcasted_iota(jnp.int32, labels.shape, 1).astype(jnp.float32)
        for start in range(0, g_class.shape[1], labels.shape[1]):
            chosen = low(jnp.where(labels == lanes + float(start), 1.0, 0.0))
            g_class[:, start : start + labels.shape[1]] = squared(mm(low_back, chosen))
        g_t2[...] = squared(mm_nt(low_back, time_all[...].reshape(D, n_dev)))
        swaps.collect(3, sums_all)
        swaps.collect(5, time_came)
        low_time = low(unpacked(jnp.sum(time_came[...], axis=0)) * silu_slope(time_one[...]))
        g_bias[15:16] = squared(mm_nt(ones, low_time)[:1])
        freqs = jnp.concatenate([rows_all[:, 1, :], rows_all[:, 2, :]], axis=1)
        g_t1[...] = squared(mm(low_time, low(freqs)))

    total = len(pieces)
    plan = [(RS_EXTRAS[0], final_step), (RS_EXTRAS[1], cond_step), (RS_EXTRAS[2], time_step)]
    for piece in range(total):
        share, when = piece * 12.0 / total, -100.0
        plan.append((RS_BEGIN[0] * share + RS_BEGIN[1], partial(begin, piece)))
        for (slope, first), step in zip(RS_PLAN, (by_core, by_far, by_near, by_line)):
            when = max(when + 0.1, slope * share + first)
            plan.append((when, partial(step, piece)))
    packed_sum, branch_sum, up_sum, down_sum, embed_sum, patch, out_rows, last_rows = sum_rows
    small_part[0:1] = packed_sum[:, :D]
    small_part[1:2] = packed_sum[:, 2 * D :]
    small_part[2:3] = branch_sum[...]
    for i in range(4):
        small_part[3 + i : 4 + i] = up_sum[:, D * i : D * (i + 1)]
    small_part[7:8] = down_sum[...]
    small_part[8:9] = embed_sum[...]
    small_part[9:25] = patch[...]
    small_part[25:41] = out_rows[...]
    small_part[41:48] = last_rows[...]
    small_part[48:56] = mods_low[...].astype(jnp.float32)
    small_part[56:64] = jnp.zeros((8, D), jnp.float32)
    for other in range(n_dev):
        own = slice(other * part, (other + 1) * part)
        groups = [small_part[r : r + 16, own] for r in (0, 16, 32, 48)]
        small_mine[other] = jnp.concatenate(groups, axis=1)
    swaps.greet()
    swaps.post(2, small_mine, small_all, each=True)
    swaps.post(0, mods_low, mods_all)
    swaps.post(3, sums_mine, sums_all)
    for _, step in sorted(plan, key=lambda planned: planned[0]):
        step()
    squares_mine[...] = jnp.broadcast_to(sum(squares), squares_mine.shape)
    swaps.post(6, squares_mine, squares_all)
    sums = jnp.sum(sums_all[...], axis=0)
    lanes = lax.broadcasted_iota(jnp.int32, sums.shape, 1)
    head_sums = jnp.where((lanes >= 1) & (lanes <= PATCH), sums, 0.0)
    swaps.collect(6, squares_all)
    all_squares = jnp.sum(squares_all[...], axis=0) + jnp.sum(head_sums * head_sums)
    totals[0:1] = sums
    totals[1:2] = jnp.sqrt(all_squares)
    swaps.finish()
    for which in range(count):
        for stage, span in enumerate((from_core, from_far, from_near, from_line)):
            transfer(
                span[which], span[which], send_sem.at[which, stage], core_sem.at[0, 0], to_core
            ).wait_send()


def scatter_and_condition(parts, inputs, n_dev, pieces):
    count, part = len(parts), D // n_dev
    shards = [p.shape[3:] for p in parts]
    vmem, anywhere = pl.BlockSpec(memory_space=pltpu.VMEM), pl.BlockSpec(memory_space=pl.ANY)
    wide, narrow = jnp.float32, jnp.bfloat16
    outs = [shards[0], (part, MAIN + MODS)]
    outs += [(part, D), (part, FREQ), (part, D), (part, D), (part, D)]
    outs += [(48, part), (19, part), (2, 128)]
    return pl.pallas_call(
        partial(scatter_kernel, pieces, count, n_dev),
        out_shape=[jax.ShapeDtypeStruct(s, wide) for s in outs],
        in_specs=[anywhere] * count + [vmem] * len(inputs),
        out_specs=[vmem] * len(outs),
        scratch_shapes=[
            pltpu.VMEM((n_dev, 8, D), narrow),
            pltpu.VMEM((n_dev, 16, 128), wide),
            pltpu.VMEM((n_dev, 16, 128), wide),
            pltpu.VMEM((1, 128), wide),
            pltpu.VMEM((n_dev, 1, 128), wide),
            pltpu.VMEM((n_dev, 1, 128), wide),
            pltpu.VMEM((64, D), wide),
            *(pltpu.VMEM((n_dev, 8, 128), wide) for _ in range(4)),
            pltpu.VMEM((n_dev, 8, D), wide),
            pltpu.VMEM((n_dev, MODS), narrow),
            pltpu.VMEM((part, n_dev), narrow),
            *(
                pltpu.VMEM((*blocks, *s), narrow)
                for blocks in ((4, LINE), (4, LINE), (2, LINE), (LINE,), (LINE - 1,))
                for s in shards
            ),
            pltpu.SemaphoreType.DMA((count, 4)),
            pltpu.SemaphoreType.DMA((len(pieces), 4)),
            pltpu.SemaphoreType.DMA((len(pieces),)),
            pltpu.SemaphoreType.DMA((len(pieces),)),
            pltpu.SemaphoreType.DMA((len(pieces), LINE - 1)),
            pltpu.SemaphoreType.DMA((len(pieces), 4)),
            pltpu.SemaphoreType.DMA((7,)),
            pltpu.SemaphoreType.DMA((7,)),
        ],
        compiler_params=pltpu.CompilerParams(
            collective_id=1, has_side_effects=True, vmem_limit_bytes=58 * 2**20
        ),
    )(*parts, *inputs)


AG_START = (4.0, -9.0)
AG_OTHERS = (4.0, -8.5)
AG_HOP = 4.25
AG_PLAN = ((4.0, 0.0), (5.0, 2.0), (5.0, 4.0), (8.5, 8.0))
AG_EXTRAS = (10.0, 25.0, 45.0, 70.0)
RS_BEGIN = (8.5, -12.0)
RS_PLAN = ((8.5, 0.0), (8.5, 6.5), (8.5, 13.0), (8.5, 19.5))
RS_EXTRAS = (12.0, 30.0, 60.0)
AG_LATE = 4
AG_SIDES = (-9.5, 5.0, 6.0, 12.0)
AG_RING = (20.0, 14.0, 6.0)
AG_CUT = 512
RS_CUT = 512


def tiled(n_dev):
    return n_dev == 8 * LINE and (D // n_dev) % 16 == 0


def column_cuts(which, columns, step):
    return [(which, (slice(None), slice(c, c + step))) for c in range(0, columns, step)]


def row_cuts(which, rows, step):
    return [(which, (slice(r, r + step), slice(None))) for r in range(0, rows, step)]


def first_part(wide, narrow, small, row, table_t, bias_t, n_dev):
    class_t, t1_t, t2_t, fs_t, fc_t = table_t
    if tiled(n_dev):
        pieces = row_cuts(1, FF // n_dev, AG_CUT // 32) + column_cuts(0, MAIN, AG_CUT)
        inputs = [wide, narrow, jnp.concatenate(jnp.split(small, 4), axis=1), row, class_t, t1_t, t2_t, fs_t, fc_t, bias_t]
        out = gather_and_condition(inputs, n_dev, tuple(pieces))
        main_all, narrow_all, *rest = out
        return [main_all.reshape(D, MAIN), narrow_all.reshape(FF, D), *rest]
    main_all = lax.all_gather(low(wide[:, :MAIN]), BOTH, axis=0, tiled=True)
    narrow_all = lax.all_gather(low(narrow), BOTH, axis=0, tiled=True)
    ada = low(wide[:, MAIN:])
    small_all = lax.all_gather(small, BOTH, axis=1, tiled=True)
    own_row = lax.dynamic_index_in_dim(row, lax.axis_index('seq'), 0, False)
    rows_all = lax.all_gather(own_row, BOTH)
    freqs = low(rows_all[:, 1:3].reshape(n_dev, FREQ))
    time_one = mm_nt(t1_t, freqs) + bias_t[:, 15:16]
    time_all = lax.all_gather(low(jax.nn.silu(time_one)), BOTH)
    classes = jnp.arange(class_t.shape[1], dtype=jnp.int32).astype(jnp.float32)
    choose = low(rows_all[:, 0, :1] == classes)
    condition = (
        mm(t2_t, time_all.reshape(D, n_dev)) + bias_t[:, 16:17] + mm_nt(class_t, choose)
    )
    cond_mine = low(jax.nn.silu(condition))
    cond_all = lax.all_gather(cond_mine, BOTH)
    mods_mine = low(mm_tn(cond_mine, ada)).reshape(n_dev, MODS // 128, 128)
    mods_came = lax.all_to_all(mods_mine, BOTH, 0, 0, tiled=True)
    mods_sum = jnp.sum(mods_came.astype(jnp.float32), axis=0)
    acts = cond_all.reshape(D, n_dev)
    both_t = [mm(fs_t, acts) + bias_t[:, 17:18], mm(fc_t, acts) + bias_t[:, 18:19]]
    final_mine = jnp.concatenate(both_t, axis=0).T[:, None]
    final_came = lax.all_to_all(final_mine, BOTH, 0, 0, tiled=True)
    return [main_all, narrow_all, small_all, rows_all, time_one, time_all, condition, cond_all, mods_sum, final_came, ada, own_row]


def last_part(parts, mods_row, sum_rows, sums_mine, ada, table_t, condition, time_one, cond_all, time_all, rows_all, n_dev):
    _, _, t2_t, fs_t, fc_t = table_t
    mods_low = low(mods_row)
    if tiled(n_dev):
        blocks = [p.reshape(LINE, LINE, 2, p.shape[0] // n_dev, p.shape[1]) for p in parts]
        pieces = row_cuts(0, FF // n_dev, RS_CUT // 32)
        for which in range(1, len(parts)):
            pieces += column_cuts(which, parts[which].shape[1], RS_CUT)
        inputs = [*sum_rows, mods_low, sums_mine, ada, fs_t, fc_t, t2_t, condition, time_one]
        inputs += [cond_all, time_all, rows_all]
        return scatter_and_condition(blocks, inputs, n_dev, tuple(pieces))
    part = D // n_dev
    shards = [
        lax.psum_scatter(p, BOTH, scatter_dimension=0, tiled=True).astype(jnp.float32) for p in parts
    ]

    def by_owner(rows):
        cut = jnp.transpose(rows.reshape(rows.shape[0], n_dev, part), (1, 0, 2))
        return lax.all_to_all(cut, BOTH, 0, 0, tiled=True)

    mods_all = lax.all_gather(mods_low, BOTH).reshape(n_dev, 8 * D)[:, :MODS]
    cut_all = by_owner(mods_low.astype(jnp.float32))
    sum_rows = [sum_rows[0][:, :D], sum_rows[0][:, 2 * D :], *sum_rows[1:]]
    small_part = jnp.concatenate([rows.reshape(-1, D) for rows in sum_rows], axis=0)
    small_sum = jnp.sum(by_owner(small_part), axis=0)
    sums = jnp.sum(lax.all_gather(sums_mine, BOTH), axis=0)
    shift, scale = low(cut_all[:, 6]), low(cut_all[:, 7])
    back = mm(shift, fs_t) + mm(scale, fc_t)
    back = lax.all_to_all(back.T.reshape(n_dev, part, n_dev), BOTH, 0, 0, tiled=True)
    back = jnp.sum(back, axis=0) + mm_nt(ada, mods_all)
    grad_cond = low(back * silu_slope(condition))
    back = mm_tn(t2_t, grad_cond).reshape(n_dev, part, n_dev)
    back = jnp.sum(lax.all_to_all(back, BOTH, 0, 0, tiled=True), axis=0)
    grad_time = low(back * silu_slope(time_one))
    acts = cond_all.reshape(D, n_dev)
    me_cond = lax.dynamic_index_in_dim(cond_all, lax.axis_index(BOTH), 0, keepdims=False)
    classes = jnp.arange(D, dtype=jnp.int32).astype(jnp.float32)
    grads = [
        shards[0],
        jnp.concatenate([shards[3], shards[2], shards[1], mm(me_cond, mods_all)], axis=1),
        mm(grad_cond, low(rows_all[:, 0, :1] == classes)),
        mm(grad_time, low(rows_all[:, 1:3].reshape(n_dev, FREQ))),
        mm_nt(grad_cond, time_all.reshape(D, n_dev)),
        mm(shift.T, acts.T),
        mm(scale.T, acts.T),
        small_sum,
    ]
    cut_sum = jnp.sum(cut_all, axis=0)
    row_of = lambda grad: jnp.sum(grad, axis=1, dtype=jnp.float32)[None]
    bias_rest = [cut_sum, row_of(grad_time), row_of(grad_cond)]
    squares = sum(jnp.sum(g * g) for g in grads + bias_rest)
    squares = jnp.sum(lax.all_gather(squares[None], BOTH)) + jnp.sum(jnp.square(sums[:, 1 : PATCH + 1]))
    g_bias = jnp.concatenate(
        [small_sum[:8], cut_sum[:6], small_sum[8:9], bias_rest[1], bias_rest[2], cut_sum[6:]], axis=0
    )
    return [*grads, g_bias, jnp.concatenate([sums, jnp.full_like(sums, jnp.sqrt(squares))], axis=0)]


def shards(
    latents,
    noises,
    labels,
    dropped,
    timesteps,
    layer_in,
    layer_out,
    cond_table,
    bias_rows,
    head_bias,
    layer_in_m,
    layer_in_v,
    layer_out_m,
    layer_out_v,
    cond_table_m,
    cond_table_v,
    bias_rows_m,
    bias_rows_v,
    head_bias_m,
    head_bias_v,
    adam_step,
):
    core = lax.axis_index("seq")
    chips = lax.axis_size("dp")
    n_dev = chips * lax.axis_size("seq")
    me = lax.axis_index("dp") * 2 + core
    norm_count = float(MICRO * chips * TOKENS_IMG * PATCH)
    part = layer_in.shape[1]

    pair = jnp.concatenate([latents[:, 0], noises[:, 0]], axis=2)
    other = lax.dynamic_index_in_dim(pair, 1 - core, 0, keepdims=False)
    mine = lax.dynamic_index_in_dim(pair, core, 0, keepdims=False)
    came = lax.ppermute(other, "seq", [(0, 1), (1, 0)])
    image = jnp.where(core == 0, jnp.concatenate([mine, came]), jnp.concatenate([came, mine]))
    latent, noise = image[:, :PATCH], image[:, PATCH:]

    classes_own = jnp.where(dropped == 1, CLASSES, labels).astype(jnp.float32)
    freqs_own = low(time_features(timesteps[:, 0])).astype(jnp.float32)
    levels_own = jnp.stack(signal_levels(timesteps[:, 0]), axis=1)
    row = jnp.concatenate(
        [
            jnp.broadcast_to(classes_own[:, :, None], (MICRO, 1, 128)),
            freqs_own.reshape(MICRO, 2, 128),
            jnp.broadcast_to(levels_own[:, :, None], (MICRO, 2, 128)),
            jnp.zeros((MICRO, 3, 128)),
        ],
        axis=1,
    )

    table_t = low(cond_table.T)
    bias_low = low(bias_rows)
    bias_t = bias_low.astype(jnp.float32).T

    small = jnp.concatenate(
        [bias_low, table_t[:, END_T2:END_PATCH].T, table_t[:, END_FINAL:].T, jnp.zeros((13, part), jnp.bfloat16)],
        axis=0,
    )
    table_parts = (
        jnp.pad(table_t[:, :END_CLASS], ((0, 0), (0, D - END_CLASS))),
        table_t[:, END_CLASS:END_T1],
        table_t[:, END_T1:END_T2],
        table_t[:, END_PATCH : END_PATCH + D],
        table_t[:, END_PATCH + D : END_FINAL],
    )
    (
        main_all,
        narrow_all,
        small_all,
        rows_all,
        time_one,
        time_all,
        condition,
        cond_all,
        mods_sum,
        final_came,
        ada_low,
        own_row,
    ) = first_part(layer_in[0], layer_out[0], small, row, table_parts, bias_t, n_dev)
    bias_all = small_all[:19].astype(jnp.float32)
    patch_w = small_all[19:35]
    out_w = small_all[35:51]
    mods = (
        mods_sum.reshape(1, MODS)
        + bias_all[8:14].reshape(1, MODS)
    )
    f_shift = final_came[:, 0, :part].reshape(1, D)
    f_scale = final_came[:, 0, part:].reshape(1, D)
    shift_a, scale_a, gate_a, shift_b, scale_b, gate_b = jnp.split(mods, 6, axis=1)

    keep_level, spread = own_row[3:4, :PATCH], own_row[4:5, :PATCH]
    noisy = low(keep_level * latent + spread * noise)
    hidden = mm(noisy, patch_w) + bias_all[14] + positions()
    unit_a, inv_a = norm_stats(hidden)
    normed_a = low(unit_a * (1.0 + scale_a) + shift_a)
    bias_qkv = jnp.concatenate([bias_all[0], jnp.zeros((D,), jnp.float32), bias_all[1]])
    packed = low(mm(normed_a, main_all[:, : 3 * D]) + bias_qkv)
    queries, keys, values = (heads_of(packed[:, i * D : (i + 1) * D]) for i in range(3))
    head_scale = 1.0 / math.sqrt(HEAD_DIM)
    scores = (
        jnp.einsum("shd,khd->hsk", queries, keys, preferred_element_type=jnp.float32) * head_scale
    )
    expd = jnp.exp(scores - jnp.max(scores, axis=-1, keepdims=True))
    probs = expd / jnp.sum(expd, axis=-1, keepdims=True)
    probs_low = low(probs)
    attended = jnp.einsum("hsk,khd->shd", probs_low, values, preferred_element_type=jnp.float32)
    attended = low(attended.reshape(TOKENS_IMG, D))
    branch = mm(attended, main_all[:, 3 * D : 4 * D]) + bias_all[2]
    middle = hidden + gate_a * branch
    unit_b, inv_b = norm_stats(middle)
    normed_b = low(unit_b * (1.0 + scale_b) + shift_b)
    upward = mm(normed_b, main_all[:, 4 * D :]) + bias_all[3:7].reshape(FF)
    activated, slope = gelu_both(upward)
    activated = low(activated)
    downward = mm(activated, narrow_all) + bias_all[7]
    last = middle + gate_b * downward
    unit_f, inv_f = norm_stats(last)
    normed_f = low(unit_f * (1.0 + f_scale) + f_shift)
    predicted = mm_nt(normed_f, out_w) + head_bias

    differ = predicted - noise
    loss_part = jnp.sum(differ * differ) / norm_count
    grad_pred = low(2.0 * differ / norm_count)
    head_part = jnp.sum(grad_pred, axis=0, dtype=jnp.float32)
    grad_out_w = mm_tn(grad_pred, normed_f)
    grad_last, g_fshift, g_fscale = norm_back(mm(grad_pred, out_w), unit_f, inv_f, f_scale)
    g_gate_b = jnp.sum(grad_last * downward, axis=0, keepdims=True)
    grad_down = low(gate_b * grad_last)
    grad_narrow = low(mm_tn(activated, grad_down))
    grad_up = low(slope * mm_nt(grad_down, narrow_all))
    grad_fc1 = low(mm_tn(normed_b, grad_up))
    grad_mid, g_shift_b, g_scale_b = norm_back(
        mm_nt(grad_up, main_all[:, 4 * D :]), unit_b, inv_b, scale_b
    )
    grad_middle = grad_last + grad_mid
    g_gate_a = jnp.sum(grad_middle * branch, axis=0, keepdims=True)
    grad_branch = low(gate_a * grad_middle)
    grad_proj = low(mm_tn(attended, grad_branch))
    grad_att = heads_of(low(mm_nt(grad_branch, main_all[:, 3 * D : 4 * D])))
    grad_probs = jnp.einsum("shd,khd->hsk", grad_att, values, preferred_element_type=jnp.float32)
    grad_values = jnp.einsum("hsk,shd->khd", probs_low, grad_att, preferred_element_type=jnp.float32)
    grad_scores = low(
        probs * (grad_probs - jnp.sum(grad_probs * probs, axis=-1, keepdims=True))
    )
    grad_queries = (
        jnp.einsum("hsk,khd->shd", grad_scores, keys, preferred_element_type=jnp.float32)
        * head_scale
    )
    grad_keys = (
        jnp.einsum("hsk,shd->khd", grad_scores, queries, preferred_element_type=jnp.float32)
        * head_scale
    )
    grad_packed = low(
        jnp.concatenate(
            [g.reshape(TOKENS_IMG, D) for g in (grad_queries, grad_keys, grad_values)], axis=1
        )
    )
    grad_qkv = low(mm_tn(normed_a, grad_packed))
    grad_hid, g_shift_a, g_scale_a = norm_back(
        mm_nt(grad_packed, main_all[:, : 3 * D]), unit_a, inv_a, scale_a
    )
    grad_embed = low(grad_middle + grad_hid)
    grad_patch = mm_tn(noisy, grad_embed)

    row_sums = lambda values: jnp.sum(values.astype(jnp.float32), axis=0, keepdims=True)
    sum_rows = [
        row_sums(grad_packed),
        row_sums(grad_branch),
        row_sums(grad_up),
        row_sums(grad_down),
        row_sums(grad_embed),
        grad_patch,
        grad_out_w,
        jnp.zeros((7, D)),
    ]
    sums_mine = jnp.pad(jnp.concatenate([loss_part[None], head_part]), (0, 111))[None]
    mods_row = low(
        jnp.concatenate(
            [g_shift_a, g_scale_a, g_gate_a, g_shift_b, g_scale_b, g_gate_b, g_fshift, g_fscale],
            axis=0,
        )
    )
    (
        grad_narrow,
        grad_wide,
        grad_class,
        grad_t1,
        grad_t2,
        grad_fs,
        grad_fc,
        small_sum,
        grad_bias,
        totals,
    ) = last_part(
        [grad_narrow, grad_fc1, grad_proj, grad_qkv],
        mods_row,
        sum_rows,
        sums_mine,
        ada_low,
        table_parts,
        condition,
        time_one,
        cond_all,
        time_all,
        rows_all,
        n_dev,
    )
    loss_total, head_total = totals[0, 0], totals[0, 1 : PATCH + 1]
    grad_table = jnp.concatenate(
        [
            grad_class[:, :END_CLASS],
            grad_t1,
            grad_t2,
            small_sum[9:25].T,
            grad_fs,
            grad_fc,
            small_sum[25:41].T,
        ],
        axis=1,
    ).T
    grad_wide, grad_narrow = grad_wide[None], grad_narrow[None]
    norm = totals[1, 0]
    factor = jnp.minimum(1.0, clip_limit / (norm + 1e-06))
    step_count = adam_step[0].astype(jnp.float32)
    results = [loss_total, norm]
    results.extend(adam(layer_in, grad_wide, layer_in_m, layer_in_v, factor, step_count))
    results.extend(adam(layer_out, grad_narrow, layer_out_m, layer_out_v, factor, step_count))
    results.extend(adam(cond_table, grad_table, cond_table_m, cond_table_v, factor, step_count))
    results.extend(adam(bias_rows, grad_bias, bias_rows_m, bias_rows_v, factor, step_count))
    results.extend(adam(head_bias, head_total, head_bias_m, head_bias_v, factor, step_count))
    return tuple(results)


def solution(mesh):
    in_specs = (
        P(None, "dp", "seq", None),
        P(None, "dp", "seq", None),
        P(None, "dp"),
        P(None, "dp"),
        P(None, "dp"),
        P(None, ("dp", "seq"), None),
        P(None, ("dp", "seq"), None),
        P(None, ("dp", "seq")),
        P(None, ("dp", "seq")),
        P(),
        P(None, ("dp", "seq"), None),
        P(None, ("dp", "seq"), None),
        P(None, ("dp", "seq"), None),
        P(None, ("dp", "seq"), None),
        P(None, ("dp", "seq")),
        P(None, ("dp", "seq")),
        P(None, ("dp", "seq")),
        P(None, ("dp", "seq")),
        P(),
        P(),
        P(),
    )
    out_specs = (
        P(),
        P(),
        P(None, ("dp", "seq"), None),
        P(None, ("dp", "seq"), None),
        P(None, ("dp", "seq"), None),
        P(None, ("dp", "seq"), None),
        P(None, ("dp", "seq"), None),
        P(None, ("dp", "seq"), None),
        P(None, ("dp", "seq")),
        P(None, ("dp", "seq")),
        P(None, ("dp", "seq")),
        P(None, ("dp", "seq")),
        P(None, ("dp", "seq")),
        P(None, ("dp", "seq")),
        P(),
        P(),
        P(),
    )
    return jax.shard_map(shards, mesh=mesh, in_specs=in_specs, out_specs=out_specs, check_vma=False)
```
